512 devices in a mesh: dp: 8 (over z_lo), seq: 64 (over x, y, z_hi, core).
Axes of the slice: x: 4, y: 4, z: 16 (z_hi: 2, z_lo: 8; z = z_hi * 8 + z_lo), core: 2. Of those that a mesh axis runs over, the one named last changes fastest.
Arguments:
- queries: bfloat16 [65536, 2048], P(('dp', 'seq')), may hold values from -8 to 8
- keys: bfloat16 [65536, 1024], P(('dp', 'seq')), may hold values from -15 to 15
- values: bfloat16 [65536, 1024], P(('dp', 'seq')), may hold values from -6 to 6
- output_gradient: bfloat16 [65536, 2048], P(('dp', 'seq')), may hold values from -6 to 6
- doc_lengths: int32 [512], replicated, may hold values from 1 to 512, 65536 in all
Outputs:
- attended: bfloat16 [65536, 2048], P(('dp', 'seq'))
- q_grad: float32 [65536, 2048], P(('dp', 'seq'))
- k_grad: float32 [65536, 1024], P(('dp', 'seq'))
- v_grad: float32 [65536, 1024], P(('dp', 'seq'))
The draws below stay inside these ranges and needn't reach their ends.
Inputs may be any that keep to these rules, and one draw needn't show every extreme that they name: `doc_lengths`: the documents fill all 65536 positions of the sequence in order, and the longest has exactly 512 tokens.
All inputs are finite; a program needn't handle non-finite values.
Results may differ from the reference program's by a relative error of at most 0.04.
Values may be sent and summed in bfloat16 or wider, within the bound.
A program may use at most 64 MiB of HBM per device.

```python
import math
import jax
import jax.numpy as jnp
import numpy as np
from jax import lax

QUERY_HEADS = 16
KEY_VALUE_HEADS = 8
HEAD_SIZE = 128
LOCAL_WINDOW = 256
PACKED_TOKENS = 65536
DOCS = 512
MOST = 512


def draw_queries(key, part):
    noise_seed, scale_seed = jax.random.split(jax.random.fold_in(key, 3))
    base_offset = jax.random.truncated_normal(noise_seed, -3.0, 3.0, (PACKED_TOKENS, QUERY_HEADS, HEAD_SIZE), jnp.float32)
    scale_values = jnp.exp(jax.random.uniform(scale_seed, (PACKED_TOKENS, QUERY_HEADS, 1), jnp.float32, jnp.log(0.5), jnp.log(2.0)))
    final_result = base_offset * scale_values
    return final_result.reshape(PACKED_TOKENS, QUERY_HEADS * HEAD_SIZE).astype(jnp.bfloat16)


def draw_keys(key, part):
    noise_seed, scale_seed = jax.random.split(jax.random.fold_in(key, 5))
    base_offset = jax.random.truncated_normal(noise_seed, -3.0, 3.0, (PACKED_TOKENS, KEY_VALUE_HEADS, HEAD_SIZE), jnp.float32)
    scale_values = jnp.exp(jax.random.uniform(scale_seed, (PACKED_TOKENS, KEY_VALUE_HEADS, 1), jnp.float32, jnp.log(0.5), jnp.log(5.0)))
    final_result = base_offset * scale_values
    return final_result.reshape(PACKED_TOKENS, KEY_VALUE_HEADS * HEAD_SIZE).astype(jnp.bfloat16)


def block_scale(stream_key, extent, pieces, least, largest):
    factor_of, own = 1.0, jax.random.fold_in(stream_key, 6)
    for dim, blocks in pieces:
        heights = jnp.exp(jax.random.uniform(jax.random.fold_in(own, dim), (blocks,), jnp.float32, least / len(pieces), largest / len(pieces)))
        factor_of = factor_of * jnp.repeat(heights, extent[dim] // blocks).reshape([-1 if axis == dim else 1 for axis in range(len(extent))])
    return factor_of


def profile(amount, total, limit, skew):
    loads = [(1 << 20) // math.isqrt(grade ** skew) + 1 for grade in range(2, amount + 1)]
    surplus, given = total - limit - (amount - 1), [1] * (amount - 1)
    while surplus > 0:
        movable = [i for i in range(amount - 1) if given[i] < limit]
        mass, budget = sum([loads[i] for i in movable]), surplus
        for i in movable:
            extra = min(limit - given[i], max(1, budget * loads[i] // mass), surplus)
            given[i] = given[i] + extra
            surplus = surplus - extra
    return np.array([limit] + given)


def uneven_parts(own_key, number_of, total, bound, slope):
    if number_of == 2:
        one = jax.random.randint(own_key, (), max(1, total - bound), min(bound, total - 1) + 1)
        return jnp.stack([one, total - one])
    tallies = jnp.asarray(profile(number_of, total, bound, slope), jnp.int32)
    couples = (number_of - 1) // 2
    source_of, taker = tallies[1:1 + 2 * couples:2], tallies[2:2 + 2 * couples:2]
    room = jnp.minimum(source_of - 1, bound - taker)
    moved = jax.random.randint(jax.random.fold_in(own_key, 1), (couples,), 0, 1 << 20) % (room + 1)
    tallies = tallies.at[1:1 + 2 * couples:2].set(source_of - moved).at[2:2 + 2 * couples:2].set(taker + moved)
    return tallies[jax.random.permutation(jax.random.fold_in(own_key, 2), number_of)]


def bell_draw(rng, shape, deviation, most, shards=(), held_as=jnp.bfloat16):
    loudness = block_scale(rng, shape, shards, -0.22, 0.18) if shards else 1.0
    values = jax.random.normal(rng, shape, jnp.float32) * deviation * loudness
    return jnp.minimum(jnp.maximum(values, -most), most).astype(held_as)


def setup_inputs(seed: int = 0) -> dict:
    streams_of = jax.random.split(jax.random.key(seed), 6)
    return {
        "queries": draw_queries(jax.random.fold_in(streams_of[5], 71), 0),
        "keys": draw_keys(jax.random.fold_in(streams_of[5], 71), 0),
        "values": bell_draw(streams_of[2], (PACKED_TOKENS, KEY_VALUE_HEADS * HEAD_SIZE), 1.0, 6.0, ((0, 512),)),
        "output_gradient": bell_draw(streams_of[3], (PACKED_TOKENS, QUERY_HEADS * HEAD_SIZE), 1.0, 6.0, ((0, 512),)),
        "doc_lengths": uneven_parts(streams_of[4], DOCS, PACKED_TOKENS, MOST, 2).astype(jnp.int32),
    }


score_scale = 168.0 ** -0.5


def doc_index(positions, doc_ends):
    doc_count = jnp.sum((doc_ends[None, :] <= positions[:, None]).astype(jnp.int32), axis=1)
    return jnp.where(positions < 0, -1, doc_count).astype(jnp.int32)


def live_pairs(query_pos, key_pos, doc_ends):
    spacing = query_pos[:, None] - key_pos[None, :]
    same_doc = doc_index(query_pos, doc_ends)[:, None] == doc_index(key_pos, doc_ends)[None, :]
    return same_doc & (spacing >= 0) & (spacing < LOCAL_WINDOW)


def reference(queries, keys, values, output_gradient, doc_lengths):
    query_groups = QUERY_HEADS // KEY_VALUE_HEADS
    rows_per_block = 256
    span_length = rows_per_block + LOCAL_WINDOW
    doc_ends = jnp.cumsum(doc_lengths).astype(jnp.int32)
    padding_amount = jnp.zeros((LOCAL_WINDOW, KEY_VALUE_HEADS * HEAD_SIZE), keys.dtype)
    key_padding = jnp.concatenate([padding_amount, keys], axis=0)
    value_padding = jnp.concatenate([padding_amount, values], axis=0)

    def one_block(number, carry):
        attended, q_grad, padded_keys, padded_values = carry
        start_index = (number * rows_per_block).astype(jnp.int32)
        heads_of_queries = lax.dynamic_slice_in_dim(queries, start_index, rows_per_block, 0).astype(jnp.float32).reshape(rows_per_block, KEY_VALUE_HEADS, query_groups, HEAD_SIZE)
        head_gradients = lax.dynamic_slice_in_dim(output_gradient, start_index, rows_per_block, 0).astype(jnp.float32).reshape(rows_per_block, KEY_VALUE_HEADS, query_groups, HEAD_SIZE)
        heads_of_keys = lax.dynamic_slice_in_dim(key_padding, start_index, span_length, 0).astype(jnp.float32).reshape(span_length, KEY_VALUE_HEADS, HEAD_SIZE)
        heads_of_values = lax.dynamic_slice_in_dim(value_padding, start_index, span_length, 0).astype(jnp.float32).reshape(span_length, KEY_VALUE_HEADS, HEAD_SIZE)
        query_pos = start_index + jnp.arange(rows_per_block, dtype=jnp.int32)
        key_pos = start_index - LOCAL_WINDOW + jnp.arange(span_length, dtype=jnp.int32)
        live_mask = live_pairs(query_pos, key_pos, doc_ends)
        scores = jnp.einsum("qgrd,kgd->grqk", heads_of_queries, heads_of_keys) * score_scale
        scores = jnp.where(live_mask[None, None], scores, -jnp.inf)
        row_max = jnp.max(scores, axis=-1)
        row_total = jnp.sum(jnp.exp(scores - row_max[..., None]), axis=-1)
        log_total = row_max + jnp.log(row_total)
        probs_full = jnp.exp(scores - log_total[..., None])
        weights = lax.optimization_barrier(probs_full.astype(jnp.bfloat16)).astype(jnp.float32)
        context_rows = jnp.einsum("grqk,kgd->qgrd", weights, heads_of_values).astype(jnp.bfloat16)
        context_wide = context_rows.astype(jnp.float32)
        grad_dot = jnp.transpose(jnp.sum(head_gradients * context_wide, axis=-1), (1, 2, 0))
        prob_grad = jnp.einsum("qgrd,kgd->grqk", head_gradients, heads_of_values)
        score_grad = (probs_full * (prob_grad - grad_dot[..., None]) * score_scale).astype(jnp.bfloat16)
        score_grad = lax.optimization_barrier(score_grad).astype(jnp.float32)
        query_part = jnp.einsum("grqk,kgd->qgrd", score_grad, heads_of_keys)
        key_portion = jnp.einsum("grqk,qgrd->kgd", score_grad, heads_of_queries)
        value_portion = jnp.einsum("grqk,qgrd->kgd", weights, head_gradients)
        attended = lax.dynamic_update_slice_in_dim(attended, context_rows.reshape(rows_per_block, QUERY_HEADS * HEAD_SIZE), start_index, 0)
        q_grad = lax.dynamic_update_slice_in_dim(q_grad, query_part.reshape(rows_per_block, QUERY_HEADS * HEAD_SIZE), start_index, 0)
        prior_keys = lax.dynamic_slice_in_dim(padded_keys, start_index, span_length, 0)
        padded_keys = lax.dynamic_update_slice_in_dim(padded_keys, prior_keys + key_portion.reshape(span_length, KEY_VALUE_HEADS * HEAD_SIZE), start_index, 0)
        prior_values = lax.dynamic_slice_in_dim(padded_values, start_index, span_length, 0)
        padded_values = lax.dynamic_update_slice_in_dim(padded_values, prior_values + value_portion.reshape(span_length, KEY_VALUE_HEADS * HEAD_SIZE), start_index, 0)
        return attended, q_grad, padded_keys, padded_values

    initial = (jnp.zeros((PACKED_TOKENS, QUERY_HEADS * HEAD_SIZE), jnp.bfloat16), jnp.zeros((PACKED_TOKENS, QUERY_HEADS * HEAD_SIZE), jnp.float32),
               jnp.zeros((PACKED_TOKENS + LOCAL_WINDOW, KEY_VALUE_HEADS * HEAD_SIZE), jnp.float32), jnp.zeros((PACKED_TOKENS + LOCAL_WINDOW, KEY_VALUE_HEADS * HEAD_SIZE), jnp.float32))
    attended, q_grad, padded_keys, padded_values = lax.fori_loop(0, PACKED_TOKENS // rows_per_block, one_block, initial)
    return attended, q_grad, padded_keys[LOCAL_WINDOW:], padded_values[LOCAL_WINDOW:]
```

```python
import jax
import jax.numpy as jnp
from jax import lax
from jax.experimental import pallas as pl
from jax.experimental.pallas import tpu as pltpu
from jax.sharding import PartitionSpec as P

HEAD = 128
ROWS = 128
CHIP_ROWS = 2 * ROWS
GROUPS = 4
QCOLS = 1024
KCOLS = 512
SCALE = 168.0 ** (-0.5)
MASKED = -1e30
MESH = pl.DeviceIdType.MESH
F32 = jnp.float32
BF16 = jnp.bfloat16


def dot_nn(a, b):
    return lax.dot_general(a, b, (((1,), (0,)), ((), ())), preferred_element_type=F32)


def dot_nt(a, b):
    return lax.dot_general(a, b, (((1,), (1,)), ((), ())), preferred_element_type=F32)


def dot_tn(a, b):
    return lax.dot_general(a, b, (((0,), (0,)), ((), ())), preferred_element_type=F32)


def make_kernel(dp_size, seq_size):
    chips = dp_size * seq_size // 2

    def place(chip, core):
        rank = chip * 2 + core
        return {"dp": rank // seq_size, "seq": lax.rem(rank, seq_size)}

    def kernel(
        q_ref, k_ref, v_ref, do_ref, len_ref,
        att_o, dq_o, dk_o, dv_o,
        qw, dow, kw, vw, halo, bias,
        att_st, dq_st, kv_full, kv_sib, ret_st, ret, out_st,
        in_l, in_s, in_r, halo_s, halo_r, ret_s, ret_r,
        res_l, res_s, res_r, fin,
    ):
        rank = lax.axis_index("dp") * seq_size + lax.axis_index("seq")
        chip = rank // 2
        core = lax.rem(rank, 2)
        other = 1 - core
        nxt = lax.rem(chip + 1, chips)
        prv = lax.rem(chip + chips - 1, chips)
        sibling = place(chip, other)
        mine = pl.multiple_of(core * ROWS, ROWS)
        theirs = pl.multiple_of(other * ROWS, ROWS)

        barrier = pltpu.get_barrier_semaphore()
        for peer in (sibling, place(nxt, 0), place(nxt, 1), place(prv, 0), place(prv, 1)):
            pl.semaphore_signal(barrier, inc=1, device_id=peer, device_id_type=MESH)

        operands = ((q_ref, qw, QCOLS), (do_ref, dow, QCOLS), (k_ref, kw, KCOLS), (v_ref, vw, KCOLS))

        def own_copy(i):
            src, dst, cols = operands[i]
            return pltpu.make_async_copy(
                src.at[:, pl.ds(pl.multiple_of(core * cols, cols), cols)],
                dst.at[pl.ds(mine, ROWS)], in_l.at[i])

        def sib_copy(i, rows):
            src, dst, cols = operands[i]
            return pltpu.make_async_remote_copy(
                src_ref=src.at[:, pl.ds(pl.multiple_of(other * cols, cols), cols)],
                dst_ref=dst.at[pl.ds(rows, ROWS)],
                send_sem=in_s.at[i], recv_sem=in_r.at[i],
                device_id=sibling, device_id_type=MESH)

        def halo_copy(g, dest, kv, rows, slot):
            src = (k_ref, v_ref)[kv]
            return pltpu.make_async_remote_copy(
                src_ref=src.at[:, pl.ds(pl.multiple_of(dest * KCOLS + g * HEAD, HEAD), HEAD)],
                dst_ref=halo.at[kv, g, pl.ds(rows, ROWS)],
                send_sem=halo_s.at[g, dest, kv], recv_sem=halo_r.at[g, slot, kv],
                device_id=place(nxt, dest), device_id_type=MESH)

        def ret_copy(g, dest, kv, slot):
            return pltpu.make_async_remote_copy(
                src_ref=ret_st.at[kv, g, pl.ds(dest * ROWS, ROWS)],
                dst_ref=ret.at[kv, slot, g],
                send_sem=ret_s.at[g, dest, kv], recv_sem=ret_r.at[g, slot, kv],
                device_id=place(prv, dest), device_id_type=MESH)

        def res_pairs(g, rows, half):
            cols = pl.multiple_of(half * QCOLS + g * 2 * HEAD, 2 * HEAD)
            return (
                (att_st.at[g, pl.ds(rows, ROWS)], att_o.at[:, pl.ds(cols, 2 * HEAD)]),
                (dq_st.at[g, pl.ds(rows, ROWS)], dq_o.at[:, pl.ds(cols, 2 * HEAD)]),
                (kv_full.at[0, g, pl.ds(rows, ROWS)], kv_sib.at[0, g]),
                (kv_full.at[1, g, pl.ds(rows, ROWS)], kv_sib.at[1, g]),
            )

        def res_remote(g, i, half):
            src, dst = res_pairs(g, theirs, half)[i]
            return pltpu.make_async_remote_copy(
                src_ref=src, dst_ref=dst, send_sem=res_s.at[g, i], recv_sem=res_r.at[g, i],
                device_id=sibling, device_id_type=MESH)

        def res_local(g, i):
            src, dst = res_pairs(g, mine, core)[i]
            return pltpu.make_async_copy(src, dst, res_l.at[g, i])

        for i in range(4):
            own_copy(i).start()
        pl.semaphore_wait(barrier, 5)

        def send_halo(g):
            for kv in range(2):
                for dest in range(2):
                    halo_copy(g, dest, kv, mine, core).start()

        send_halo(0)
        for i in range(4):
            sib_copy(i, mine).start()

        @pl.loop(1, GROUPS)
        def _(g):
            send_halo(g)

        lane = lax.broadcasted_iota(jnp.int32, (8, 512), 1)
        ends = jnp.broadcast_to(len_ref[...], (8, 512)).astype(F32)
        step = 1
        while step < 512:
            ends = ends + jnp.where(lane >= step, pltpu.roll(ends, step, 1), 0.0)
            step *= 2
        base = (chip * CHIP_ROWS).astype(F32)
        row = lax.broadcasted_iota(jnp.int32, (CHIP_ROWS, CHIP_ROWS), 0)
        col = lax.broadcasted_iota(jnp.int32, (CHIP_ROWS, CHIP_ROWS), 1)
        position = lax.broadcasted_iota(jnp.int32, (CHIP_ROWS, 512), 0).astype(F32) + base
        ends_b = jnp.broadcast_to(ends[0:1], (CHIP_ROWS, 512))
        first = jnp.max(jnp.where(ends_b <= position, ends_b, 0.0), axis=1, keepdims=True) - base
        own = col <= row
        key_pos = jnp.where(own, col, col - CHIP_ROWS).astype(F32)
        bias[...] = jnp.where(key_pos >= first, 0.0, MASKED)

        for i in range(4):
            own_copy(i).wait()
        for i in range(4):
            copy = sib_copy(i, theirs)
            copy.wait_send()
            copy.wait_recv()

        @pl.loop(0, GROUPS)
        def _(g):
            for slot in range(2):
                for kv in range(2):
                    halo_copy(g, 0, kv, slot * ROWS, slot).wait_recv()
            kcols = pl.ds(pl.multiple_of(g * HEAD, HEAD), HEAD)
            k_own = kw[:, kcols]
            v_own = vw[:, kcols]
            k_halo = halo[0, g]
            v_halo = halo[1, g]
            sums = None
            for r in range(2):
                qcols = pl.ds(pl.multiple_of(g * 2 * HEAD + r * HEAD, HEAD), HEAD)
                qh = qw[:, qcols]
                gh = dow[:, qcols]
                score = jnp.where(own, dot_nt(qh, k_own), dot_nt(qh, k_halo)) * SCALE + bias[...]
                top = jnp.max(score, axis=1, keepdims=True)
                e = jnp.exp(score - top)
                prob = e / jnp.sum(e, axis=1, keepdims=True)
                w_own = jnp.where(own, prob, 0.0).astype(BF16)
                w_halo = jnp.where(own, 0.0, prob).astype(BF16)
                att = (dot_nn(w_own, v_own) + dot_nn(w_halo, v_halo)).astype(BF16)
                att_st[g, :, r * HEAD:(r + 1) * HEAD] = att
                delta = jnp.sum(gh.astype(F32) * att.astype(F32), axis=1, keepdims=True)
                dprob = jnp.where(own, dot_nt(gh, v_own), dot_nt(gh, v_halo))
                ds = prob * (dprob - delta) * SCALE
                ds_own = jnp.where(own, ds, 0.0).astype(BF16)
                ds_halo = jnp.where(own, 0.0, ds).astype(BF16)
                dq_st[g, :, r * HEAD:(r + 1) * HEAD] = dot_nn(ds_own, k_own) + dot_nn(ds_halo, k_halo)
                part = (dot_tn(ds_halo, qh), dot_tn(w_halo, gh), dot_tn(ds_own, qh), dot_tn(w_own, gh))
                sums = part if sums is None else tuple(a + b for a, b in zip(sums, part))
            ret_st[0, g] = sums[0].astype(BF16)
            ret_st[1, g] = sums[1].astype(BF16)
            for kv in range(2):
                for dest in range(2):
                    ret_copy(g, dest, kv, core).start()
            kv_full[0, g] = sums[2]
            kv_full[1, g] = sums[3]
            for i in range(4):
                res_remote(g, i, core).start()
            for i in range(2):
                res_local(g, i).start()

        def fin_copy(g, half, kv):
            cols = pl.ds(pl.multiple_of(half * KCOLS + g * HEAD, HEAD), HEAD)
            return pltpu.make_async_copy(out_st.at[kv, half, g], (dk_o, dv_o)[kv].at[:, cols], fin.at[kv, half, g])

        @pl.loop(0, GROUPS)
        def _(g):
            for i in range(4):
                copy = res_remote(g, i, other)
                copy.wait_send()
                copy.wait_recv()
            for i in range(2):
                res_local(g, i).wait()
            for kv in range(2):
                for dest in range(2):
                    halo_copy(g, dest, kv, mine, core).wait_send()
                for slot in range(2):
                    ret_copy(g, slot, kv, slot).wait_recv()
                out_st[kv, core, g] = kv_full[kv, g, pl.ds(mine, ROWS)] + ret[kv, core, g].astype(F32)
                out_st[kv, other, g] = kv_sib[kv, g] + ret[kv, other, g].astype(F32)
                fin_copy(g, core, kv).start()
                fin_copy(g, other, kv).start()

        @pl.loop(0, GROUPS)
        def _(g):
            for kv in range(2):
                for dest in range(2):
                    ret_copy(g, dest, kv, core).wait_send()
                for half in range(2):
                    fin_copy(g, half, kv).wait()

    return kernel


def solution(mesh):
    dp_size, seq_size = mesh.shape["dp"], mesh.shape["seq"]
    kernel = make_kernel(dp_size, seq_size)
    anyspace = pl.BlockSpec(memory_space=pl.ANY)
    dma = pltpu.SemaphoreType.DMA

    def on_device(queries, keys, values, output_gradient, doc_lengths):
        return pl.pallas_call(
            kernel,
            out_shape=(
                jax.ShapeDtypeStruct((ROWS, 2048), BF16),
                jax.ShapeDtypeStruct((ROWS, 2048), F32),
                jax.ShapeDtypeStruct((ROWS, 1024), F32),
                jax.ShapeDtypeStruct((ROWS, 1024), F32),
            ),
            in_specs=[anyspace] * 4 + [pl.BlockSpec(memory_space=pltpu.VMEM)],
            out_specs=(anyspace,) * 4,
            scratch_shapes=[
                pltpu.VMEM((CHIP_ROWS, QCOLS), BF16),
                pltpu.VMEM((CHIP_ROWS, QCOLS), BF16),
                pltpu.VMEM((CHIP_ROWS, KCOLS), BF16),
                pltpu.VMEM((CHIP_ROWS, KCOLS), BF16),
                pltpu.VMEM((2, GROUPS, CHIP_ROWS, HEAD), BF16),
                pltpu.VMEM((CHIP_ROWS, CHIP_ROWS), F32),
                pltpu.VMEM((GROUPS, CHIP_ROWS, 2 * HEAD), BF16),
                pltpu.VMEM((GROUPS, CHIP_ROWS, 2 * HEAD), F32),
                pltpu.VMEM((2, GROUPS, CHIP_ROWS, HEAD), F32),
                pltpu.VMEM((2, GROUPS, ROWS, HEAD), F32),
                pltpu.VMEM((2, GROUPS, CHIP_ROWS, HEAD), BF16),
                pltpu.VMEM((2, 2, GROUPS, ROWS, HEAD), BF16),
                pltpu.VMEM((2, 2, GROUPS, ROWS, HEAD), F32),
                dma((4,)), dma((4,)), dma((4,)),
                dma((GROUPS, 2, 2)), dma((GROUPS, 2, 2)),
                dma((GROUPS, 2, 2)), dma((GROUPS, 2, 2)),
                dma((GROUPS, 2)), dma((GROUPS, 4)), dma((GROUPS, 4)),
                dma((2, 2, GROUPS)),
            ],
            compiler_params=pltpu.CompilerParams(
                collective_id=0, has_side_effects=True, vmem_limit_bytes=40 << 20),
        )(queries, keys, values, output_gradient, doc_lengths.reshape(1, -1))

    rows = P(("dp", "seq"), None)
    return jax.shard_map(
        on_device, mesh=mesh, in_specs=(rows,) * 4 + (P(),), out_specs=(rows,) * 4, check_vma=False)
```

```python
import jax
import jax.numpy as jnp
from jax import lax
from jax.experimental import pallas as pl
from jax.experimental.pallas import tpu as pltpu
from jax.sharding import PartitionSpec as P

HEAD = 128
ROWS = 128
CHIP_ROWS = 2 * ROWS
GROUPS = 4
QCOLS = 1024
KCOLS = 512
SCALE = 168.0 ** (-0.5)
MASKED = -1e30
VMEM_BYTES = 62 << 20
MESH = pl.DeviceIdType.MESH
F32 = jnp.float32
BF16 = jnp.bfloat16


def dot_nn(a, b):
    return lax.dot_general(a, b, (((1,), (0,)), ((), ())), preferred_element_type=F32)


def dot_nt(a, b):
    return lax.dot_general(a, b, (((1,), (1,)), ((), ())), preferred_element_type=F32)


def dot_tn(a, b):
    return lax.dot_general(a, b, (((0,), (0,)), ((), ())), preferred_element_type=F32)


def make_kernel(dp_size, seq_size):
    chips = dp_size * seq_size // 2
    run = seq_size // 2

    def place(chip, core):
        rank = chip * 2 + core
        return {"dp": rank // seq_size, "seq": lax.rem(rank, seq_size)}

    def kernel(
        q_ref, k_ref, v_ref, do_ref, len_ref,
        att_o, dq_o, dk_o, dv_o,
        qw, dow, kw, vw, halo, bias,
        att_st, dq_st, kv_full, kv_sib, ret_st, ret, out_st,
        pass_h, pass_r,
        in_l, in_s, in_r, halo_s, halo_r, ret_s, ret_r,
        res_l, res_s, res_r, fin, pass_hs, pass_hr, pass_rs, pass_rr,
    ):
        rank = lax.axis_index("dp") * seq_size + lax.axis_index("seq")
        chip = rank // 2
        core = lax.rem(rank, 2)
        other = 1 - core
        nxt = lax.rem(chip + 1, chips)
        prv = lax.rem(chip + chips - 1, chips)
        sibling = place(chip, other)
        mine = pl.multiple_of(core * ROWS, ROWS)
        theirs = pl.multiple_of(other * ROWS, ROWS)

        line = chip // run
        even = lax.rem(line, 2) == 0
        src_wrap = lax.rem(chip, run) == run - 1
        dst_wrap = lax.rem(chip, run) == 0
        is_last = chip == chips - 1
        is_first = chip == 0
        sends_far = src_wrap & even
        takes_far = dst_wrap & jnp.logical_not(even)
        passes_h = dst_wrap & even
        passes_r = src_wrap & jnp.logical_not(even)
        sends_near = jnp.logical_not((src_wrap & even) | is_last)
        takes_near = jnp.logical_not((dst_wrap & jnp.logical_not(even)) | is_first)
        h_way = place(lax.rem(chip + chips - run + 1, chips), core)
        r_way = place(lax.rem(chip + run - 1, chips), core)
        h_from, h_to = lax.rem(chip + run - 1, chips), lax.rem(chip + run, chips)
        r_from, r_to = lax.rem(chip + chips - run + 1, chips), lax.rem(chip + chips - run, chips)

        barrier = pltpu.get_barrier_semaphore()

        def greet(*peers):
            for peer in peers:
                pl.semaphore_signal(barrier, inc=1, device_id=peer, device_id_type=MESH)

        greet(sibling)

        @pl.when(sends_near)
        def _():
            greet(place(nxt, 0), place(nxt, 1))

        @pl.when(takes_near)
        def _():
            greet(place(prv, 0), place(prv, 1))

        @pl.when(passes_h)
        def _():
            greet(place(h_from, core), place(h_to, 0), place(h_to, 1))

        @pl.when(passes_r)
        def _():
            greet(place(r_from, core), place(r_to, 0), place(r_to, 1))

        @pl.when(sends_far)
        def _():
            back = lax.rem(chip + run, chips)
            greet(h_way, place(back, 0), place(back, 1))

        @pl.when(takes_far)
        def _():
            ahead = lax.rem(chip + chips - run, chips)
            greet(r_way, place(ahead, 0), place(ahead, 1))

        operands = ((q_ref, qw, QCOLS), (do_ref, dow, QCOLS), (k_ref, kw, KCOLS), (v_ref, vw, KCOLS))

        def own_copy(i):
            src, dst, cols = operands[i]
            return pltpu.make_async_copy(
                src.at[:, pl.ds(pl.multiple_of(core * cols, cols), cols)],
                dst.at[pl.ds(mine, ROWS)], in_l.at[i])

        def sib_copy(i, rows):
            src, dst, cols = operands[i]
            return pltpu.make_async_remote_copy(
                src_ref=src.at[:, pl.ds(pl.multiple_of(other * cols, cols), cols)],
                dst_ref=dst.at[pl.ds(rows, ROWS)],
                send_sem=in_s.at[i], recv_sem=in_r.at[i],
                device_id=sibling, device_id_type=MESH)

        def halo_src(g, dest, kv):
            return (k_ref, v_ref)[kv].at[:, pl.ds(pl.multiple_of(dest * KCOLS + g * HEAD, HEAD), HEAD)]

        def halo_copy(g, dest, kv, rows, slot):
            return pltpu.make_async_remote_copy(
                src_ref=halo_src(g, dest, kv),
                dst_ref=halo.at[kv, g, pl.ds(rows, ROWS)],
                send_sem=halo_s.at[g, dest, kv], recv_sem=halo_r.at[g, slot, kv],
                device_id=place(nxt, dest), device_id_type=MESH)

        def ret_copy(g, dest, kv, slot):
            return pltpu.make_async_remote_copy(
                src_ref=ret_st.at[kv, g, pl.ds(dest * ROWS, ROWS)],
                dst_ref=ret.at[kv, slot, g],
                send_sem=ret_s.at[g, dest, kv], recv_sem=ret_r.at[g, slot, kv],
                device_id=place(prv, dest), device_id_type=MESH)

        def res_pairs(g, rows, half):
            cols = pl.multiple_of(half * QCOLS + g * 2 * HEAD, 2 * HEAD)
            return (
                (att_st.at[g, pl.ds(rows, ROWS)], att_o.at[:, pl.ds(cols, 2 * HEAD)]),
                (dq_st.at[g, pl.ds(rows, ROWS)], dq_o.at[:, pl.ds(cols, 2 * HEAD)]),
                (kv_full.at[0, g, pl.ds(rows, ROWS)], kv_sib.at[0, g]),
                (kv_full.at[1, g, pl.ds(rows, ROWS)], kv_sib.at[1, g]),
            )

        def res_remote(g, i, half):
            src, dst = res_pairs(g, theirs, half)[i]
            return pltpu.make_async_remote_copy(
                src_ref=src, dst_ref=dst, send_sem=res_s.at[g, i], recv_sem=res_r.at[g, i],
                device_id=sibling, device_id_type=MESH)

        def res_local(g, i):
            src, dst = res_pairs(g, mine, core)[i]
            return pltpu.make_async_copy(src, dst, res_l.at[g, i])

        for i in range(4):
            own_copy(i).start()

        @pl.when(is_first)
        def _():
            halo[...] = jnp.zeros_like(halo)

        @pl.when(is_last)
        def _():
            ret[...] = jnp.zeros_like(ret)

        def far_copy(g, dest, kv):
            return pltpu.make_async_remote_copy(
                src_ref=halo_src(g, dest, kv), dst_ref=pass_h.at[g, dest, kv],
                send_sem=halo_s.at[g, dest, kv], recv_sem=pass_hr.at[g, dest, kv],
                device_id=h_way, device_id_type=MESH)

        def far_ret(g, dest, kv):
            return pltpu.make_async_remote_copy(
                src_ref=ret_st.at[kv, g, pl.ds(dest * ROWS, ROWS)], dst_ref=pass_r.at[g, dest, kv],
                send_sem=ret_s.at[g, dest, kv], recv_sem=pass_rr.at[g, dest, kv],
                device_id=r_way, device_id_type=MESH)

        def on_halo(g, dest, kv):
            return pltpu.make_async_remote_copy(
                src_ref=pass_h.at[g, dest, kv], dst_ref=halo.at[kv, g, pl.ds(mine, ROWS)],
                send_sem=pass_hs.at[g, dest, kv], recv_sem=halo_r.at[g, core, kv],
                device_id=place(h_to, dest), device_id_type=MESH)

        def on_ret(g, dest, kv):
            return pltpu.make_async_remote_copy(
                src_ref=pass_r.at[g, dest, kv], dst_ref=ret.at[kv, core, g],
                send_sem=pass_rs.at[g, dest, kv], recv_sem=ret_r.at[g, core, kv],
                device_id=place(r_to, dest), device_id_type=MESH)

        def far_arrival(buf, sem, g, dest, kv):
            return pltpu.make_async_remote_copy(
                src_ref=buf.at[g, dest, kv], dst_ref=buf.at[g, dest, kv],
                send_sem=pass_hs.at[g, dest, kv], recv_sem=sem.at[g, dest, kv],
                device_id=sibling, device_id_type=MESH)

        pieces = [(dest, kv) for kv in range(2) for dest in range(2)]
        zero = jnp.int32(0)
        expected = (
            1 + jnp.where(sends_near, 2, zero) + jnp.where(takes_near, 2, zero)
            + jnp.where(passes_h, 3, zero) + jnp.where(passes_r, 3, zero)
            + jnp.where(sends_far, 3, zero) + jnp.where(takes_far, 3, zero))
        pl.semaphore_wait(barrier, expected)

        def send_halo(g):
            @pl.when(sends_near)
            def _():
                for kv in range(2):
                    for dest in range(2):
                        halo_copy(g, dest, kv, mine, core).start()

            @pl.when(sends_far)
            def _():
                for kv in range(2):
                    for dest in range(2):
                        far_copy(g, dest, kv).start()

        send_halo(0)
        for i in range(4):
            sib_copy(i, mine).start()

        @pl.loop(1, GROUPS)
        def _(g):
            send_halo(g)

        lane = lax.broadcasted_iota(jnp.int32, (8, 512), 1)
        ends = jnp.broadcast_to(len_ref[...], (8, 512)).astype(F32)
        step = 1
        while step < 512:
            ends = ends + jnp.where(lane >= step, pltpu.roll(ends, step, 1), 0.0)
            step *= 2
        base = (chip * CHIP_ROWS).astype(F32)
        row = lax.broadcasted_iota(jnp.int32, (CHIP_ROWS, CHIP_ROWS), 0)
        col = lax.broadcasted_iota(jnp.int32, (CHIP_ROWS, CHIP_ROWS), 1)
        position = lax.broadcasted_iota(jnp.int32, (CHIP_ROWS, 512), 0).astype(F32) + base
        ends_b = jnp.broadcast_to(ends[0:1], (CHIP_ROWS, 512))
        first = jnp.max(jnp.where(ends_b <= position, ends_b, 0.0), axis=1, keepdims=True) - base
        own = col <= row
        key_pos = jnp.where(own, col, col - CHIP_ROWS).astype(F32)
        bias[...] = jnp.where(key_pos >= first, 0.0, MASKED)

        for i in range(4):
            own_copy(i).wait()
        for i in range(4):
            copy = sib_copy(i, theirs)
            copy.wait_send()
            copy.wait_recv()

        @pl.loop(0, GROUPS)
        def _(g):
            @pl.when(passes_h)
            def _():
                for dest, kv in pieces:
                    far_arrival(pass_h, pass_hr, g, dest, kv).wait_recv()
                    on_halo(g, dest, kv).start()

            @pl.when(jnp.logical_not(is_first))
            def _():
                for slot in range(2):
                    for kv in range(2):
                        halo_copy(g, 0, kv, slot * ROWS, slot).wait_recv()

            kcols = pl.ds(pl.multiple_of(g * HEAD, HEAD), HEAD)
            k_own = kw[:, kcols]
            v_own = vw[:, kcols]
            k_halo = halo[0, g]
            v_halo = halo[1, g]
            sums = None
            for r in range(2):
                qcols = pl.ds(pl.multiple_of(g * 2 * HEAD + r * HEAD, HEAD), HEAD)
                qh = qw[:, qcols]
                gh = dow[:, qcols]
                score = jnp.where(own, dot_nt(qh, k_own), dot_nt(qh, k_halo)) * SCALE + bias[...]
                top = jnp.max(score, axis=1, keepdims=True)
                e = jnp.exp(score - top)
                prob = e / jnp.sum(e, axis=1, keepdims=True)
                w_own = jnp.where(own, prob, 0.0).astype(BF16)
                w_halo = jnp.where(own, 0.0, prob).astype(BF16)
                att = (dot_nn(w_own, v_own) + dot_nn(w_halo, v_halo)).astype(BF16)
                att_st[g, :, r * HEAD:(r + 1) * HEAD] = att
                delta = jnp.sum(gh.astype(F32) * att.astype(F32), axis=1, keepdims=True)
                dprob = jnp.where(own, dot_nt(gh, v_own), dot_nt(gh, v_halo))
                ds = prob * (dprob - delta) * SCALE
                ds_own = jnp.where(own, ds, 0.0).astype(BF16)
                ds_halo = jnp.where(own, 0.0, ds).astype(BF16)
                dq_st[g, :, r * HEAD:(r + 1) * HEAD] = dot_nn(ds_own, k_own) + dot_nn(ds_halo, k_halo)
                part = (dot_tn(ds_halo, qh), dot_tn(w_halo, gh), dot_tn(ds_own, qh), dot_tn(w_own, gh))
                sums = part if sums is None else tuple(a + b for a, b in zip(sums, part))
            ret_st[0, g] = sums[0].astype(BF16)
            ret_st[1, g] = sums[1].astype(BF16)

            @pl.when(takes_near)
            def _():
                for kv in range(2):
                    for dest in range(2):
                        ret_copy(g, dest, kv, core).start()

            @pl.when(takes_far)
            def _():
                for kv in range(2):
                    for dest in range(2):
                        far_ret(g, dest, kv).start()

            kv_full[0, g] = sums[2]
            kv_full[1, g] = sums[3]
            for i in range(4):
                res_remote(g, i, core).start()
            for i in range(2):
                res_local(g, i).start()

        def fin_copy(g, half, kv):
            cols = pl.ds(pl.multiple_of(half * KCOLS + g * HEAD, HEAD), HEAD)
            return pltpu.make_async_copy(out_st.at[kv, half, g], (dk_o, dv_o)[kv].at[:, cols], fin.at[kv, half, g])

        @pl.loop(0, GROUPS)
        def _(g):
            @pl.when(passes_r)
            def _():
                for dest, kv in pieces:
                    far_arrival(pass_r, pass_rr, g, dest, kv).wait_recv()
                    on_ret(g, dest, kv).start()

            for i in range(4):
                copy = res_remote(g, i, other)
                copy.wait_send()
                copy.wait_recv()
            for i in range(2):
                res_local(g, i).wait()

            @pl.when(jnp.logical_not(is_last))
            def _():
                for kv in range(2):
                    for dest in range(2):
                        halo_copy(g, dest, kv, mine, core).wait_send()
                    for slot in range(2):
                        ret_copy(g, slot, kv, slot).wait_recv()

            for kv in range(2):
                out_st[kv, core, g] = kv_full[kv, g, pl.ds(mine, ROWS)] + ret[kv, core, g].astype(F32)
                out_st[kv, other, g] = kv_sib[kv, g] + ret[kv, other, g].astype(F32)
                fin_copy(g, core, kv).start()
                fin_copy(g, other, kv).start()

        @pl.loop(0, GROUPS)
        def _(g):
            @pl.when(jnp.logical_not(is_first))
            def _():
                for kv in range(2):
                    for dest in range(2):
                        ret_copy(g, dest, kv, core).wait_send()

            for kv in range(2):
                for half in range(2):
                    fin_copy(g, half, kv).wait()

        @pl.when(passes_h)
        def _():
            @pl.loop(0, GROUPS)
            def _(g):
                for dest, kv in pieces:
                    on_halo(g, dest, kv).wait_send()

        @pl.when(passes_r)
        def _():
            @pl.loop(0, GROUPS)
            def _(g):
                for dest, kv in pieces:
                    on_ret(g, dest, kv).wait_send()

    return kernel


def solution(mesh):
    dp_size, seq_size = mesh.shape["dp"], mesh.shape["seq"]
    kernel = make_kernel(dp_size, seq_size)
    anyspace = pl.BlockSpec(memory_space=pl.ANY)
    in_hbm = pl.BlockSpec(memory_space=pltpu.HBM)
    dma = pltpu.SemaphoreType.DMA

    def on_device(queries, keys, values, output_gradient, doc_lengths):
        return pl.pallas_call(
            kernel,
            out_shape=(
                jax.ShapeDtypeStruct((ROWS, 2048), BF16),
                jax.ShapeDtypeStruct((ROWS, 2048), F32),
                jax.ShapeDtypeStruct((ROWS, 1024), F32),
                jax.ShapeDtypeStruct((ROWS, 1024), F32),
            ),
            in_specs=[in_hbm] * 4 + [pl.BlockSpec(memory_space=pltpu.VMEM)],
            out_specs=(anyspace,) * 4,
            scratch_shapes=[
                pltpu.VMEM((CHIP_ROWS, QCOLS), BF16),
                pltpu.VMEM((CHIP_ROWS, QCOLS), BF16),
                pltpu.VMEM((CHIP_ROWS, KCOLS), BF16),
                pltpu.VMEM((CHIP_ROWS, KCOLS), BF16),
                pltpu.VMEM((2, GROUPS, CHIP_ROWS, HEAD), BF16),
                pltpu.VMEM((CHIP_ROWS, CHIP_ROWS), F32),
                pltpu.VMEM((GROUPS, CHIP_ROWS, 2 * HEAD), BF16),
                pltpu.VMEM((GROUPS, CHIP_ROWS, 2 * HEAD), F32),
                pltpu.VMEM((2, GROUPS, CHIP_ROWS, HEAD), F32),
                pltpu.VMEM((2, GROUPS, ROWS, HEAD), F32),
                pltpu.VMEM((2, GROUPS, CHIP_ROWS, HEAD), BF16),
                pltpu.VMEM((2, 2, GROUPS, ROWS, HEAD), BF16),
                pltpu.VMEM((2, 2, GROUPS, ROWS, HEAD), F32),
                pltpu.VMEM((GROUPS, 2, 2, ROWS, HEAD), BF16),
                pltpu.VMEM((GROUPS, 2, 2, ROWS, HEAD), BF16),
                dma((4,)), dma((4,)), dma((4,)),
                dma((GROUPS, 2, 2)), dma((GROUPS, 2, 2)),
                dma((GROUPS, 2, 2)), dma((GROUPS, 2, 2)),
                dma((GROUPS, 2)), dma((GROUPS, 4)), dma((GROUPS, 4)),
                dma((2, 2, GROUPS)),
                dma((GROUPS, 2, 2)), dma((GROUPS, 2, 2)), dma((GROUPS, 2, 2)), dma((GROUPS, 2, 2)),
            ],
            compiler_params=pltpu.CompilerParams(
                collective_id=0, has_side_effects=True, vmem_limit_bytes=VMEM_BYTES),
        )(queries, keys, values, output_gradient, doc_lengths.reshape(1, -1))

    rows = P(("dp", "seq"), None)
    return jax.shard_map(
        on_device, mesh=mesh, in_specs=(rows,) * 4 + (P(),), out_specs=(rows,) * 4, check_vma=False)
```

```python
import jax
import jax.numpy as jnp
from jax import lax
from jax.experimental import pallas as pl
from jax.experimental.pallas import tpu as pltpu
from jax.sharding import PartitionSpec as P

HEAD = 128
ROWS = 128
CHIP_ROWS = 2 * ROWS
GROUPS = 4
QCOLS = 1024
KCOLS = 512
SCALE = 168.0 ** (-0.5)
MASKED = -1e30
FAR = 2
VMEM_BYTES = 62 << 20
MESH = pl.DeviceIdType.MESH
F32 = jnp.float32
BF16 = jnp.bfloat16


def dot_nn(a, b):
    return lax.dot_general(a, b, (((1,), (0,)), ((), ())), preferred_element_type=F32)


def dot_nt(a, b):
    return lax.dot_general(a, b, (((1,), (1,)), ((), ())), preferred_element_type=F32)


def dot_tn(a, b):
    return lax.dot_general(a, b, (((0,), (0,)), ((), ())), preferred_element_type=F32)


def make_kernel(dp_size, seq_size):
    chips = dp_size * seq_size // 2
    run = seq_size // 2

    def place(chip, core):
        rank = chip * 2 + core
        return {"dp": rank // seq_size, "seq": lax.rem(rank, seq_size)}

    def kernel(
        q_ref, k_ref, v_ref, do_ref, len_ref,
        att_o, dq_o, dk_o, dv_o,
        qw, dow, kw, vw, halo, bias,
        att_st, dq_st, kv_full, kv_sib, ret_st, ret, out_st,
        pass_h, pass_r,
        in_l, in_s, in_r, halo_s, halo_r, ret_s, ret_r,
        res_l, res_s, res_r, fin, pass_hs, pass_hr, pass_rs, pass_rr,
    ):
        rank = lax.axis_index("dp") * seq_size + lax.axis_index("seq")
        chip = rank // 2
        core = lax.rem(rank, 2)
        other = 1 - core
        nxt = lax.rem(chip + 1, chips)
        prv = lax.rem(chip + chips - 1, chips)
        sibling = place(chip, other)
        mine = pl.multiple_of(core * ROWS, ROWS)
        theirs = pl.multiple_of(other * ROWS, ROWS)

        line = chip // run
        even = lax.rem(line, 2) == 0
        src_wrap = lax.rem(chip, run) == run - 1
        dst_wrap = lax.rem(chip, run) == 0
        is_last = chip == chips - 1
        is_first = chip == 0
        sends_far = src_wrap & even & (line >= FAR)
        takes_far = dst_wrap & jnp.logical_not(even) & (line >= FAR)
        passes_h = dst_wrap & even & (line >= FAR)
        passes_r = src_wrap & jnp.logical_not(even) & (line >= FAR)
        sends_near = jnp.logical_not(sends_far | is_last)
        takes_near = jnp.logical_not(takes_far | is_first)
        h_way = place(lax.rem(chip + chips - run + 1, chips), core)
        r_way = place(lax.rem(chip + run - 1, chips), core)
        h_from, h_to = lax.rem(chip + run - 1, chips), lax.rem(chip + run, chips)
        r_from, r_to = lax.rem(chip + chips - run + 1, chips), lax.rem(chip + chips - run, chips)

        barrier = pltpu.get_barrier_semaphore()

        def greet(*peers):
            for peer in peers:
                pl.semaphore_signal(barrier, inc=1, device_id=peer, device_id_type=MESH)

        greet(sibling)

        @pl.when(sends_near)
        def _():
            greet(place(nxt, 0), place(nxt, 1))

        @pl.when(takes_near)
        def _():
            greet(place(prv, 0), place(prv, 1))

        @pl.when(passes_h)
        def _():
            greet(place(h_from, core), place(h_to, 0), place(h_to, 1))

        @pl.when(passes_r)
        def _():
            greet(place(r_from, core), place(r_to, 0), place(r_to, 1))

        @pl.when(sends_far)
        def _():
            back = lax.rem(chip + run, chips)
            greet(h_way, place(back, 0), place(back, 1))

        @pl.when(takes_far)
        def _():
            ahead = lax.rem(chip + chips - run, chips)
            greet(r_way, place(ahead, 0), place(ahead, 1))

        operands = ((q_ref, qw, QCOLS), (do_ref, dow, QCOLS), (k_ref, kw, KCOLS), (v_ref, vw, KCOLS))

        def own_copy(i):
            src, dst, cols = operands[i]
            return pltpu.make_async_copy(
                src.at[:, pl.ds(pl.multiple_of(core * cols, cols), cols)],
                dst.at[pl.ds(mine, ROWS)], in_l.at[i])

        def sib_copy(i, rows):
            src, dst, cols = operands[i]
            return pltpu.make_async_remote_copy(
                src_ref=src.at[:, pl.ds(pl.multiple_of(other * cols, cols), cols)],
                dst_ref=dst.at[pl.ds(rows, ROWS)],
                send_sem=in_s.at[i], recv_sem=in_r.at[i],
                device_id=sibling, device_id_type=MESH)

        def halo_src(g, dest, kv):
            return (k_ref, v_ref)[kv].at[:, pl.ds(pl.multiple_of(dest * KCOLS + g * HEAD, HEAD), HEAD)]

        def halo_copy(g, dest, kv, rows, slot):
            return pltpu.make_async_remote_copy(
                src_ref=halo_src(g, dest, kv),
                dst_ref=halo.at[kv, g, pl.ds(rows, ROWS)],
                send_sem=halo_s.at[g, dest, kv], recv_sem=halo_r.at[g, slot, kv],
                device_id=place(nxt, dest), device_id_type=MESH)

        def ret_copy(g, dest, kv, slot):
            return pltpu.make_async_remote_copy(
                src_ref=ret_st.at[kv, g, pl.ds(dest * ROWS, ROWS)],
                dst_ref=ret.at[kv, slot, g],
                send_sem=ret_s.at[g, dest, kv], recv_sem=ret_r.at[g, slot, kv],
                device_id=place(prv, dest), device_id_type=MESH)

        def res_pairs(g, rows, half):
            cols = pl.multiple_of(half * QCOLS + g * 2 * HEAD, 2 * HEAD)
            return (
                (att_st.at[g, pl.ds(rows, ROWS)], att_o.at[:, pl.ds(cols, 2 * HEAD)]),
                (dq_st.at[g, pl.ds(rows, ROWS)], dq_o.at[:, pl.ds(cols, 2 * HEAD)]),
                (kv_full.at[0, g, pl.ds(rows, ROWS)], kv_sib.at[0, g]),
                (kv_full.at[1, g, pl.ds(rows, ROWS)], kv_sib.at[1, g]),
            )

        def res_remote(g, i, half):
            src, dst = res_pairs(g, theirs, half)[i]
            return pltpu.make_async_remote_copy(
                src_ref=src, dst_ref=dst, send_sem=res_s.at[g, i], recv_sem=res_r.at[g, i],
                device_id=sibling, device_id_type=MESH)

        def res_local(g, i):
            src, dst = res_pairs(g, mine, core)[i]
            return pltpu.make_async_copy(src, dst, res_l.at[g, i])

        for i in range(4):
            own_copy(i).start()

        @pl.when(is_first)
        def _():
            halo[...] = jnp.zeros_like(halo)

        @pl.when(is_last)
        def _():
            ret[...] = jnp.zeros_like(ret)

        def far_copy(g, dest, kv):
            return pltpu.make_async_remote_copy(
                src_ref=halo_src(g, dest, kv), dst_ref=pass_h.at[g, dest, kv],
                send_sem=halo_s.at[g, dest, kv], recv_sem=pass_hr.at[g, dest, kv],
                device_id=h_way, device_id_type=MESH)

        def far_ret(g, dest, kv):
            return pltpu.make_async_remote_copy(
                src_ref=ret_st.at[kv, g, pl.ds(dest * ROWS, ROWS)], dst_ref=pass_r.at[g, dest, kv],
                send_sem=ret_s.at[g, dest, kv], recv_sem=pass_rr.at[g, dest, kv],
                device_id=r_way, device_id_type=MESH)

        def on_halo(g, dest, kv):
            return pltpu.make_async_remote_copy(
                src_ref=pass_h.at[g, dest, kv], dst_ref=halo.at[kv, g, pl.ds(mine, ROWS)],
                send_sem=pass_hs.at[g, dest, kv], recv_sem=halo_r.at[g, core, kv],
                device_id=place(h_to, dest), device_id_type=MESH)

        def on_ret(g, dest, kv):
            return pltpu.make_async_remote_copy(
                src_ref=pass_r.at[g, dest, kv], dst_ref=ret.at[kv, core, g],
                send_sem=pass_rs.at[g, dest, kv], recv_sem=ret_r.at[g, core, kv],
                device_id=place(r_to, dest), device_id_type=MESH)

        def far_arrival(buf, sem, g, dest, kv):
            return pltpu.make_async_remote_copy(
                src_ref=buf.at[g, dest, kv], dst_ref=buf.at[g, dest, kv],
                send_sem=pass_hs.at[g, dest, kv], recv_sem=sem.at[g, dest, kv],
                device_id=sibling, device_id_type=MESH)

        pieces = [(dest, kv) for kv in range(2) for dest in range(2)]
        zero = jnp.int32(0)
        expected = (
            1 + jnp.where(sends_near, 2, zero) + jnp.where(takes_near, 2, zero)
            + jnp.where(passes_h, 3, zero) + jnp.where(passes_r, 3, zero)
            + jnp.where(sends_far, 3, zero) + jnp.where(takes_far, 3, zero))
        pl.semaphore_wait(barrier, expected)

        def send_halo(g):
            @pl.when(sends_near)
            def _():
                for kv in range(2):
                    for dest in range(2):
                        halo_copy(g, dest, kv, mine, core).start()

            @pl.when(sends_far)
            def _():
                for kv in range(2):
                    for dest in range(2):
                        far_copy(g, dest, kv).start()

        send_halo(0)
        for i in range(4):
            sib_copy(i, mine).start()

        @pl.loop(1, GROUPS)
        def _(g):
            send_halo(g)

        lane = lax.broadcasted_iota(jnp.int32, (8, 512), 1)
        ends = jnp.broadcast_to(len_ref[...], (8, 512)).astype(F32)
        step = 1
        while step < 512:
            ends = ends + jnp.where(lane >= step, pltpu.roll(ends, step, 1), 0.0)
            step *= 2
        base = (chip * CHIP_ROWS).astype(F32)
        row = lax.broadcasted_iota(jnp.int32, (CHIP_ROWS, CHIP_ROWS), 0)
        col = lax.broadcasted_iota(jnp.int32, (CHIP_ROWS, CHIP_ROWS), 1)
        position = lax.broadcasted_iota(jnp.int32, (CHIP_ROWS, 512), 0).astype(F32) + base
        ends_b = jnp.broadcast_to(ends[0:1], (CHIP_ROWS, 512))
        first = jnp.max(jnp.where(ends_b <= position, ends_b, 0.0), axis=1, keepdims=True) - base
        own = col <= row
        key_pos = jnp.where(own, col, col - CHIP_ROWS).astype(F32)
        bias[...] = jnp.where(key_pos >= first, 0.0, MASKED)

        for i in range(4):
            own_copy(i).wait()
        for i in range(4):
            copy = sib_copy(i, theirs)
            copy.wait_send()
            copy.wait_recv()

        @pl.loop(0, GROUPS)
        def _(g):
            @pl.when(passes_h)
            def _():
                for dest, kv in pieces:
                    far_arrival(pass_h, pass_hr, g, dest, kv).wait_recv()
                    on_halo(g, dest, kv).start()

            @pl.when(jnp.logical_not(is_first))
            def _():
                for slot in range(2):
                    for kv in range(2):
                        halo_copy(g, 0, kv, slot * ROWS, slot).wait_recv()

            kcols = pl.ds(pl.multiple_of(g * HEAD, HEAD), HEAD)
            k_own = kw[:, kcols]
            v_own = vw[:, kcols]
            k_halo = halo[0, g]
            v_halo = halo[1, g]
            sums = None
            for r in range(2):
                qcols = pl.ds(pl.multiple_of(g * 2 * HEAD + r * HEAD, HEAD), HEAD)
                qh = qw[:, qcols]
                gh = dow[:, qcols]
                score = jnp.where(own, dot_nt(qh, k_own), dot_nt(qh, k_halo)) * SCALE + bias[...]
                top = jnp.max(score, axis=1, keepdims=True)
                e = jnp.exp(score - top)
                prob = e / jnp.sum(e, axis=1, keepdims=True)
                w_own = jnp.where(own, prob, 0.0).astype(BF16)
                w_halo = jnp.where(own, 0.0, prob).astype(BF16)
                att = (dot_nn(w_own, v_own) + dot_nn(w_halo, v_halo)).astype(BF16)
                att_st[g, :, r * HEAD:(r + 1) * HEAD] = att
                delta = jnp.sum(gh.astype(F32) * att.astype(F32), axis=1, keepdims=True)
                dprob = jnp.where(own, dot_nt(gh, v_own), dot_nt(gh, v_halo))
                ds = prob * (dprob - delta) * SCALE
                ds_own = jnp.where(own, ds, 0.0).astype(BF16)
                ds_halo = jnp.where(own, 0.0, ds).astype(BF16)
                dq_st[g, :, r * HEAD:(r + 1) * HEAD] = dot_nn(ds_own, k_own) + dot_nn(ds_halo, k_halo)
                part = (dot_tn(ds_halo, qh), dot_tn(w_halo, gh), dot_tn(ds_own, qh), dot_tn(w_own, gh))
                sums = part if sums is None else tuple(a + b for a, b in zip(sums, part))
            ret_st[0, g] = sums[0].astype(BF16)
            ret_st[1, g] = sums[1].astype(BF16)

            @pl.when(takes_near)
            def _():
                for kv in range(2):
                    for dest in range(2):
                        ret_copy(g, dest, kv, core).start()

            @pl.when(takes_far)
            def _():
                for kv in range(2):
                    for dest in range(2):
                        far_ret(g, dest, kv).start()

            kv_full[0, g] = sums[2]
            kv_full[1, g] = sums[3]
            for i in range(4):
                res_remote(g, i, core).start()
            for i in range(2):
                res_local(g, i).start()

        @pl.when(passes_r)
        def _():
            @pl.loop(0, GROUPS)
            def _(g):
                for dest, kv in pieces:
                    far_arrival(pass_r, pass_rr, g, dest, kv).wait_recv()
                    on_ret(g, dest, kv).start()

        def fin_copy(g, half, kv):
            cols = pl.ds(pl.multiple_of(half * KCOLS + g * HEAD, HEAD), HEAD)
            return pltpu.make_async_copy(out_st.at[kv, half, g], (dk_o, dv_o)[kv].at[:, cols], fin.at[kv, half, g])

        @pl.loop(0, GROUPS)
        def _(g):
            for i in range(4):
                copy = res_remote(g, i, other)
                copy.wait_send()
                copy.wait_recv()
            for i in range(2):
                res_local(g, i).wait()

            @pl.when(jnp.logical_not(is_last))
            def _():
                for kv in range(2):
                    for dest in range(2):
                        halo_copy(g, dest, kv, mine, core).wait_send()
                    for slot in range(2):
                        ret_copy(g, slot, kv, slot).wait_recv()

            for kv in range(2):
                out_st[kv, core, g] = kv_full[kv, g, pl.ds(mine, ROWS)] + ret[kv, core, g].astype(F32)
                out_st[kv, other, g] = kv_sib[kv, g] + ret[kv, other, g].astype(F32)
                fin_copy(g, core, kv).start()
                fin_copy(g, other, kv).start()

        @pl.loop(0, GROUPS)
        def _(g):
            @pl.when(jnp.logical_not(is_first))
            def _():
                for kv in range(2):
                    for dest in range(2):
                        ret_copy(g, dest, kv, core).wait_send()

            for kv in range(2):
                for half in range(2):
                    fin_copy(g, half, kv).wait()

        @pl.when(passes_h)
        def _():
            @pl.loop(0, GROUPS)
            def _(g):
                for dest, kv in pieces:
                    on_halo(g, dest, kv).wait_send()

        @pl.when(passes_r)
        def _():
            @pl.loop(0, GROUPS)
            def _(g):
                for dest, kv in pieces:
                    on_ret(g, dest, kv).wait_send()

    return kernel


def hand_over(*refs):
    sources, targets, holds, sem_in, sem_out = refs[:4], refs[4:8], refs[8:12], refs[12], refs[13]
    parts = [(i, p) for p in range(4) for i in range(4)]

    def take(i, p):
        rows = pl.ds(p * (ROWS // 4), ROWS // 4)
        return pltpu.make_async_copy(sources[i].at[rows], holds[i].at[rows], sem_in.at[i, p])

    def give(i, p):
        rows = pl.ds(p * (ROWS // 4), ROWS // 4)
        return pltpu.make_async_copy(holds[i].at[rows], targets[i].at[rows], sem_out.at[i, p])

    for part in parts:
        take(*part).start()
    for part in parts:
        take(*part).wait()
        give(*part).start()
    for part in parts:
        give(*part).wait()


def solution(mesh):
    dp_size, seq_size = mesh.shape["dp"], mesh.shape["seq"]
    kernel = make_kernel(dp_size, seq_size)
    anyspace = pl.BlockSpec(memory_space=pl.ANY)
    in_hbm = pl.BlockSpec(memory_space=pltpu.HBM)
    dma = pltpu.SemaphoreType.DMA

    def on_device(queries, keys, values, output_gradient, doc_lengths):
        results = (
            jax.ShapeDtypeStruct((ROWS, 2048), BF16),
            jax.ShapeDtypeStruct((ROWS, 2048), F32),
            jax.ShapeDtypeStruct((ROWS, 1024), F32),
            jax.ShapeDtypeStruct((ROWS, 1024), F32),
        )
        found = pl.pallas_call(
            kernel,
            out_shape=results,
            in_specs=[in_hbm] * 4 + [pl.BlockSpec(memory_space=pltpu.VMEM)],
            out_specs=(anyspace,) * 4,
            scratch_shapes=[
                pltpu.VMEM((CHIP_ROWS, QCOLS), BF16),
                pltpu.VMEM((CHIP_ROWS, QCOLS), BF16),
                pltpu.VMEM((CHIP_ROWS, KCOLS), BF16),
                pltpu.VMEM((CHIP_ROWS, KCOLS), BF16),
                pltpu.VMEM((2, GROUPS, CHIP_ROWS, HEAD), BF16),
                pltpu.VMEM((CHIP_ROWS, CHIP_ROWS), F32),
                pltpu.VMEM((GROUPS, CHIP_ROWS, 2 * HEAD), BF16),
                pltpu.VMEM((GROUPS, CHIP_ROWS, 2 * HEAD), F32),
                pltpu.VMEM((2, GROUPS, CHIP_ROWS, HEAD), F32),
                pltpu.VMEM((2, GROUPS, ROWS, HEAD), F32),
                pltpu.VMEM((2, GROUPS, CHIP_ROWS, HEAD), BF16),
                pltpu.VMEM((2, 2, GROUPS, ROWS, HEAD), BF16),
                pltpu.VMEM((2, 2, GROUPS, ROWS, HEAD), F32),
                pltpu.VMEM((GROUPS, 2, 2, ROWS, HEAD), BF16),
                pltpu.VMEM((GROUPS, 2, 2, ROWS, HEAD), BF16),
                dma((4,)), dma((4,)), dma((4,)),
                dma((GROUPS, 2, 2)), dma((GROUPS, 2, 2)),
                dma((GROUPS, 2, 2)), dma((GROUPS, 2, 2)),
                dma((GROUPS, 2)), dma((GROUPS, 4)), dma((GROUPS, 4)),
                dma((2, 2, GROUPS)),
                dma((GROUPS, 2, 2)), dma((GROUPS, 2, 2)), dma((GROUPS, 2, 2)), dma((GROUPS, 2, 2)),
            ],
            compiler_params=pltpu.CompilerParams(
                collective_id=0, has_side_effects=True, vmem_limit_bytes=VMEM_BYTES),
        )(queries, keys, values, output_gradient, doc_lengths.reshape(1, -1))
        return pl.pallas_call(
            hand_over,
            out_shape=results,
            in_specs=[in_hbm] * 4,
            out_specs=(in_hbm,) * 4,
            scratch_shapes=[pltpu.VMEM(r.shape, r.dtype) for r in results] + [dma((4, 4)), dma((4, 4))],
            compiler_params=pltpu.CompilerParams(vmem_limit_bytes=VMEM_BYTES),
        )(*found)

    rows = P(("dp", "seq"), None)
    return jax.shard_map(
        on_device, mesh=mesh, in_specs=(rows,) * 4 + (P(),), out_specs=(rows,) * 4, check_vma=False)
```

```python
import jax
import jax.numpy as jnp
from jax import lax
from jax.experimental import pallas as pl
from jax.experimental.pallas import tpu as pltpu
from jax.sharding import PartitionSpec as P

HEAD = 128
ROWS = 128
CHIP_ROWS = 2 * ROWS
GROUPS = 4
QCOLS = 1024
KCOLS = 512
SCALE = 168.0 ** (-0.5)
MASKED = -1e30
FAR = 2
FAR_BACK = 0
VMEM_BYTES = 62 << 20
MESH = pl.DeviceIdType.MESH
F32 = jnp.float32
BF16 = jnp.bfloat16


def dot_nn(a, b):
    return lax.dot_general(a, b, (((1,), (0,)), ((), ())), preferred_element_type=F32)


def dot_nt(a, b):
    return lax.dot_general(a, b, (((1,), (1,)), ((), ())), preferred_element_type=F32)


def dot_tn(a, b):
    return lax.dot_general(a, b, (((0,), (0,)), ((), ())), preferred_element_type=F32)


def make_kernel(dp_size, seq_size):
    chips = dp_size * seq_size // 2
    run = seq_size // 2

    def place(chip, core):
        rank = chip * 2 + core
        return {"dp": rank // seq_size, "seq": lax.rem(rank, seq_size)}

    def kernel(
        q_ref, k_ref, v_ref, do_ref, len_ref,
        att_o, dq_o, dk_o, dv_o,
        qw, dow, kw, vw, halo, bias,
        att_st, dq_st, kv_full, kv_sib, ret_st, ret, out_st,
        pass_h, pass_r,
        in_l, in_s, in_r, halo_s, halo_r, ret_s, ret_r,
        res_l, res_s, res_r, fin, pass_hs, pass_hr, pass_rs, pass_rr,
    ):
        rank = lax.axis_index("dp") * seq_size + lax.axis_index("seq")
        chip = rank // 2
        core = lax.rem(rank, 2)
        other = 1 - core
        nxt = lax.rem(chip + 1, chips)
        prv = lax.rem(chip + chips - 1, chips)
        sibling = place(chip, other)
        mine = pl.multiple_of(core * ROWS, ROWS)
        theirs = pl.multiple_of(other * ROWS, ROWS)

        line = chip // run
        even = lax.rem(line, 2) == 0
        src_wrap = lax.rem(chip, run) == run - 1
        dst_wrap = lax.rem(chip, run) == 0
        is_last = chip == chips - 1
        is_first = chip == 0
        sends_far = src_wrap & even & (line >= FAR)
        takes_far = dst_wrap & jnp.logical_not(even) & (line >= FAR_BACK)
        gets_far = dst_wrap & jnp.logical_not(even) & (line >= FAR)
        owed_far = src_wrap & even & (line >= FAR_BACK)
        passes_h = dst_wrap & even & (line >= FAR)
        passes_r = src_wrap & jnp.logical_not(even) & (line >= FAR_BACK)
        sends_near = jnp.logical_not(sends_far | is_last)
        takes_near = jnp.logical_not(takes_far | is_first)
        h_way = place(lax.rem(chip + chips - run + 1, chips), core)
        r_way = place(lax.rem(chip + run - 1, chips), core)
        h_from, h_to = lax.rem(chip + run - 1, chips), lax.rem(chip + run, chips)
        r_from, r_to = lax.rem(chip + chips - run + 1, chips), lax.rem(chip + chips - run, chips)

        barrier = pltpu.get_barrier_semaphore()

        def greet(*peers):
            for peer in peers:
                pl.semaphore_signal(barrier, inc=1, device_id=peer, device_id_type=MESH)

        greet(sibling)

        meets_nxt = jnp.logical_not(is_last | (sends_far & owed_far))
        meets_prv = jnp.logical_not(is_first | (takes_far & gets_far))

        @pl.when(meets_nxt)
        def _():
            greet(place(nxt, 0), place(nxt, 1))

        @pl.when(meets_prv)
        def _():
            greet(place(prv, 0), place(prv, 1))

        @pl.when(passes_h)
        def _():
            greet(place(h_from, core), place(h_to, 0), place(h_to, 1))

        @pl.when(passes_r)
        def _():
            greet(place(r_from, core), place(r_to, 0), place(r_to, 1))

        @pl.when(sends_far)
        def _():
            greet(h_way)

        @pl.when(owed_far)
        def _():
            back = lax.rem(chip + run, chips)
            greet(place(back, 0), place(back, 1))

        @pl.when(takes_far)
        def _():
            greet(r_way)

        @pl.when(gets_far)
        def _():
            ahead = lax.rem(chip + chips - run, chips)
            greet(place(ahead, 0), place(ahead, 1))

        operands = ((q_ref, qw, QCOLS), (do_ref, dow, QCOLS), (k_ref, kw, KCOLS), (v_ref, vw, KCOLS))

        def own_copy(i):
            src, dst, cols = operands[i]
            return pltpu.make_async_copy(
                src.at[:, pl.ds(pl.multiple_of(core * cols, cols), cols)],
                dst.at[pl.ds(mine, ROWS)], in_l.at[i])

        def sib_copy(i, rows):
            src, dst, cols = operands[i]
            return pltpu.make_async_remote_copy(
                src_ref=src.at[:, pl.ds(pl.multiple_of(other * cols, cols), cols)],
                dst_ref=dst.at[pl.ds(rows, ROWS)],
                send_sem=in_s.at[i], recv_sem=in_r.at[i],
                device_id=sibling, device_id_type=MESH)

        def halo_src(g, dest, kv):
            return (k_ref, v_ref)[kv].at[:, pl.ds(pl.multiple_of(dest * KCOLS + g * HEAD, HEAD), HEAD)]

        def halo_copy(g, dest, kv, rows, slot):
            return pltpu.make_async_remote_copy(
                src_ref=halo_src(g, dest, kv),
                dst_ref=halo.at[kv, g, pl.ds(rows, ROWS)],
                send_sem=halo_s.at[g, dest, kv], recv_sem=halo_r.at[g, slot, kv],
                device_id=place(nxt, dest), device_id_type=MESH)

        def ret_copy(g, dest, kv, slot):
            return pltpu.make_async_remote_copy(
                src_ref=ret_st.at[kv, g, pl.ds(dest * ROWS, ROWS)],
                dst_ref=ret.at[kv, slot, g],
                send_sem=ret_s.at[g, dest, kv], recv_sem=ret_r.at[g, slot, kv],
                device_id=place(prv, dest), device_id_type=MESH)

        def res_pairs(g, rows, half):
            cols = pl.multiple_of(half * QCOLS + g * 2 * HEAD, 2 * HEAD)
            return (
                (att_st.at[g, pl.ds(rows, ROWS)], att_o.at[:, pl.ds(cols, 2 * HEAD)]),
                (dq_st.at[g, pl.ds(rows, ROWS)], dq_o.at[:, pl.ds(cols, 2 * HEAD)]),
                (kv_full.at[0, g, pl.ds(rows, ROWS)], kv_sib.at[0, g]),
                (kv_full.at[1, g, pl.ds(rows, ROWS)], kv_sib.at[1, g]),
            )

        def res_remote(g, i, half):
            src, dst = res_pairs(g, theirs, half)[i]
            return pltpu.make_async_remote_copy(
                src_ref=src, dst_ref=dst, send_sem=res_s.at[g, i], recv_sem=res_r.at[g, i],
                device_id=sibling, device_id_type=MESH)

        def res_local(g, i):
            src, dst = res_pairs(g, mine, core)[i]
            return pltpu.make_async_copy(src, dst, res_l.at[g, i])

        for i in range(4):
            own_copy(i).start()

        @pl.when(is_first)
        def _():
            halo[...] = jnp.zeros_like(halo)

        @pl.when(is_last)
        def _():
            ret[...] = jnp.zeros_like(ret)

        def far_copy(g, dest, kv):
            return pltpu.make_async_remote_copy(
                src_ref=halo_src(g, dest, kv), dst_ref=pass_h.at[g, dest, kv],
                send_sem=halo_s.at[g, dest, kv], recv_sem=pass_hr.at[g, dest, kv],
                device_id=h_way, device_id_type=MESH)

        def far_ret(g, dest, kv):
            return pltpu.make_async_remote_copy(
                src_ref=ret_st.at[kv, g, pl.ds(dest * ROWS, ROWS)], dst_ref=pass_r.at[g, dest, kv],
                send_sem=ret_s.at[g, dest, kv], recv_sem=pass_rr.at[g, dest, kv],
                device_id=r_way, device_id_type=MESH)

        def on_halo(g, dest, kv):
            return pltpu.make_async_remote_copy(
                src_ref=pass_h.at[g, dest, kv], dst_ref=halo.at[kv, g, pl.ds(mine, ROWS)],
                send_sem=pass_hs.at[g, dest, kv], recv_sem=halo_r.at[g, core, kv],
                device_id=place(h_to, dest), device_id_type=MESH)

        def on_ret(g, dest, kv):
            return pltpu.make_async_remote_copy(
                src_ref=pass_r.at[g, dest, kv], dst_ref=ret.at[kv, core, g],
                send_sem=pass_rs.at[g, dest, kv], recv_sem=ret_r.at[g, core, kv],
                device_id=place(r_to, dest), device_id_type=MESH)

        def far_arrival(buf, sem, g, dest, kv):
            return pltpu.make_async_remote_copy(
                src_ref=buf.at[g, dest, kv], dst_ref=buf.at[g, dest, kv],
                send_sem=pass_hs.at[g, dest, kv], recv_sem=sem.at[g, dest, kv],
                device_id=sibling, device_id_type=MESH)

        pieces = [(dest, kv) for kv in range(2) for dest in range(2)]
        zero = jnp.int32(0)
        def some(count, cond):
            return jnp.where(cond, count, zero)

        expected = (
            1 + some(2, meets_nxt) + some(2, meets_prv) + some(3, passes_h) + some(3, passes_r)
            + some(1, sends_far) + some(2, owed_far) + some(1, takes_far) + some(2, gets_far))
        pl.semaphore_wait(barrier, expected)

        def send_halo(g):
            @pl.when(sends_near)
            def _():
                for kv in range(2):
                    for dest in range(2):
                        halo_copy(g, dest, kv, mine, core).start()

            @pl.when(sends_far)
            def _():
                for kv in range(2):
                    for dest in range(2):
                        far_copy(g, dest, kv).start()

        send_halo(0)
        for i in range(4):
            sib_copy(i, mine).start()

        @pl.loop(1, GROUPS)
        def _(g):
            send_halo(g)

        lane = lax.broadcasted_iota(jnp.int32, (8, 512), 1)
        ends = jnp.broadcast_to(len_ref[...], (8, 512)).astype(F32)
        step = 1
        while step < 512:
            ends = ends + jnp.where(lane >= step, pltpu.roll(ends, step, 1), 0.0)
            step *= 2
        base = (chip * CHIP_ROWS).astype(F32)
        row = lax.broadcasted_iota(jnp.int32, (CHIP_ROWS, CHIP_ROWS), 0)
        col = lax.broadcasted_iota(jnp.int32, (CHIP_ROWS, CHIP_ROWS), 1)
        position = lax.broadcasted_iota(jnp.int32, (CHIP_ROWS, 512), 0).astype(F32) + base
        ends_b = jnp.broadcast_to(ends[0:1], (CHIP_ROWS, 512))
        first = jnp.max(jnp.where(ends_b <= position, ends_b, 0.0), axis=1, keepdims=True) - base
        own = col <= row
        key_pos = jnp.where(own, col, col - CHIP_ROWS).astype(F32)
        bias[...] = jnp.where(key_pos >= first, 0.0, MASKED)

        for i in range(4):
            own_copy(i).wait()
        for i in range(4):
            copy = sib_copy(i, theirs)
            copy.wait_send()
            copy.wait_recv()

        @pl.loop(0, GROUPS)
        def _(g):
            @pl.when(passes_h & (g == 0))
            def _():
                for i in range(GROUPS):
                    for dest, kv in pieces:
                        far_arrival(pass_h, pass_hr, i, dest, kv).wait_recv()
                        on_halo(i, dest, kv).start()

            @pl.when(jnp.logical_not(is_first))
            def _():
                for slot in range(2):
                    for kv in range(2):
                        halo_copy(g, 0, kv, slot * ROWS, slot).wait_recv()

            kcols = pl.ds(pl.multiple_of(g * HEAD, HEAD), HEAD)
            k_own = kw[:, kcols]
            v_own = vw[:, kcols]
            k_halo = halo[0, g]
            v_halo = halo[1, g]
            sums = None
            for r in range(2):
                qcols = pl.ds(pl.multiple_of(g * 2 * HEAD + r * HEAD, HEAD), HEAD)
                qh = qw[:, qcols]
                gh = dow[:, qcols]
                score = jnp.where(own, dot_nt(qh, k_own), dot_nt(qh, k_halo)) * SCALE + bias[...]
                top = jnp.max(score, axis=1, keepdims=True)
                e = jnp.exp(score - top)
                prob = e / jnp.sum(e, axis=1, keepdims=True)
                w_own = jnp.where(own, prob, 0.0).astype(BF16)
                w_halo = jnp.where(own, 0.0, prob).astype(BF16)
                att = (dot_nn(w_own, v_own) + dot_nn(w_halo, v_halo)).astype(BF16)
                att_st[g, :, r * HEAD:(r + 1) * HEAD] = att
                delta = jnp.sum(gh.astype(F32) * att.astype(F32), axis=1, keepdims=True)
                dprob = jnp.where(own, dot_nt(gh, v_own), dot_nt(gh, v_halo))
                ds = prob * (dprob - delta) * SCALE
                ds_own = jnp.where(own, ds, 0.0).astype(BF16)
                ds_halo = jnp.where(own, 0.0, ds).astype(BF16)
                dq_st[g, :, r * HEAD:(r + 1) * HEAD] = dot_nn(ds_own, k_own) + dot_nn(ds_halo, k_halo)
                part = (dot_tn(ds_halo, qh), dot_tn(w_halo, gh), dot_tn(ds_own, qh), dot_tn(w_own, gh))
                sums = part if sums is None else tuple(a + b for a, b in zip(sums, part))
            ret_st[0, g] = sums[0].astype(BF16)
            ret_st[1, g] = sums[1].astype(BF16)

            @pl.when(takes_near)
            def _():
                for kv in range(2):
                    for dest in range(2):
                        ret_copy(g, dest, kv, core).start()

            @pl.when(takes_far)
            def _():
                for kv in range(2):
                    for dest in range(2):
                        far_ret(g, dest, kv).start()

            kv_full[0, g] = sums[2]
            kv_full[1, g] = sums[3]
            for i in range(4):
                res_remote(g, i, core).start()
            for i in range(2):
                res_local(g, i).start()

        @pl.when(passes_r)
        def _():
            @pl.loop(0, GROUPS)
            def _(g):
                for dest, kv in pieces:
                    far_arrival(pass_r, pass_rr, g, dest, kv).wait_recv()
                    on_ret(g, dest, kv).start()

        def fin_copy(g, half, kv):
            cols = pl.ds(pl.multiple_of(half * KCOLS + g * HEAD, HEAD), HEAD)
            return pltpu.make_async_copy(out_st.at[kv, half, g], (dk_o, dv_o)[kv].at[:, cols], fin.at[kv, half, g])

        @pl.loop(0, GROUPS)
        def _(g):
            for i in range(4):
                copy = res_remote(g, i, other)
                copy.wait_send()
                copy.wait_recv()
            for i in range(2):
                res_local(g, i).wait()

            @pl.when(jnp.logical_not(is_last))
            def _():
                for kv in range(2):
                    for dest in range(2):
                        halo_copy(g, dest, kv, mine, core).wait_send()
                    for slot in range(2):
                        ret_copy(g, slot, kv, slot).wait_recv()

            for kv in range(2):
                out_st[kv, core, g] = kv_full[kv, g, pl.ds(mine, ROWS)] + ret[kv, core, g].astype(F32)
                out_st[kv, other, g] = kv_sib[kv, g] + ret[kv, other, g].astype(F32)
                fin_copy(g, core, kv).start()
                fin_copy(g, other, kv).start()

        @pl.loop(0, GROUPS)
        def _(g):
            @pl.when(jnp.logical_not(is_first))
            def _():
                for kv in range(2):
                    for dest in range(2):
                        ret_copy(g, dest, kv, core).wait_send()

            for kv in range(2):
                for half in range(2):
                    fin_copy(g, half, kv).wait()

        @pl.when(passes_h)
        def _():
            @pl.loop(0, GROUPS)
            def _(g):
                for dest, kv in pieces:
                    on_halo(g, dest, kv).wait_send()

        @pl.when(passes_r)
        def _():
            @pl.loop(0, GROUPS)
            def _(g):
                for dest, kv in pieces:
                    on_ret(g, dest, kv).wait_send()

    return kernel


def hand_over(*refs):
    sources, targets, holds, sem_in, sem_out = refs[:4], refs[4:8], refs[8:12], refs[12], refs[13]
    parts = [(i, p) for p in range(4) for i in range(4)]

    def take(i, p):
        rows = pl.ds(p * (ROWS // 4), ROWS // 4)
        return pltpu.make_async_copy(sources[i].at[rows], holds[i].at[rows], sem_in.at[i, p])

    def give(i, p):
        rows = pl.ds(p * (ROWS // 4), ROWS // 4)
        return pltpu.make_async_copy(holds[i].at[rows], targets[i].at[rows], sem_out.at[i, p])

    for part in parts:
        take(*part).start()
    for part in parts:
        take(*part).wait()
        give(*part).start()
    for part in parts:
        give(*part).wait()


def solution(mesh):
    dp_size, seq_size = mesh.shape["dp"], mesh.shape["seq"]
    kernel = make_kernel(dp_size, seq_size)
    anyspace = pl.BlockSpec(memory_space=pl.ANY)
    in_hbm = pl.BlockSpec(memory_space=pltpu.HBM)
    dma = pltpu.SemaphoreType.DMA

    def on_device(queries, keys, values, output_gradient, doc_lengths):
        results = (
            jax.ShapeDtypeStruct((ROWS, 2048), BF16),
            jax.ShapeDtypeStruct((ROWS, 2048), F32),
            jax.ShapeDtypeStruct((ROWS, 1024), F32),
            jax.ShapeDtypeStruct((ROWS, 1024), F32),
        )
        found = pl.pallas_call(
            kernel,
            out_shape=results,
            in_specs=[in_hbm] * 4 + [pl.BlockSpec(memory_space=pltpu.VMEM)],
            out_specs=(anyspace,) * 4,
            scratch_shapes=[
                pltpu.VMEM((CHIP_ROWS, QCOLS), BF16),
                pltpu.VMEM((CHIP_ROWS, QCOLS), BF16),
                pltpu.VMEM((CHIP_ROWS, KCOLS), BF16),
                pltpu.VMEM((CHIP_ROWS, KCOLS), BF16),
                pltpu.VMEM((2, GROUPS, CHIP_ROWS, HEAD), BF16),
                pltpu.VMEM((CHIP_ROWS, CHIP_ROWS), F32),
                pltpu.VMEM((GROUPS, CHIP_ROWS, 2 * HEAD), BF16),
                pltpu.VMEM((GROUPS, CHIP_ROWS, 2 * HEAD), F32),
                pltpu.VMEM((2, GROUPS, CHIP_ROWS, HEAD), F32),
                pltpu.VMEM((2, GROUPS, ROWS, HEAD), F32),
                pltpu.VMEM((2, GROUPS, CHIP_ROWS, HEAD), BF16),
                pltpu.VMEM((2, 2, GROUPS, ROWS, HEAD), BF16),
                pltpu.VMEM((2, 2, GROUPS, ROWS, HEAD), F32),
                pltpu.VMEM((GROUPS, 2, 2, ROWS, HEAD), BF16),
                pltpu.VMEM((GROUPS, 2, 2, ROWS, HEAD), BF16),
                dma((4,)), dma((4,)), dma((4,)),
                dma((GROUPS, 2, 2)), dma((GROUPS, 2, 2)),
                dma((GROUPS, 2, 2)), dma((GROUPS, 2, 2)),
                dma((GROUPS, 2)), dma((GROUPS, 4)), dma((GROUPS, 4)),
                dma((2, 2, GROUPS)),
                dma((GROUPS, 2, 2)), dma((GROUPS, 2, 2)), dma((GROUPS, 2, 2)), dma((GROUPS, 2, 2)),
            ],
            compiler_params=pltpu.CompilerParams(
                collective_id=0, has_side_effects=True, vmem_limit_bytes=VMEM_BYTES),
        )(queries, keys, values, output_gradient, doc_lengths.reshape(1, -1))
        return pl.pallas_call(
            hand_over,
            out_shape=results,
            in_specs=[in_hbm] * 4,
            out_specs=(in_hbm,) * 4,
            scratch_shapes=[pltpu.VMEM(r.shape, r.dtype) for r in results] + [dma((4, 4)), dma((4, 4))],
            compiler_params=pltpu.CompilerParams(vmem_limit_bytes=VMEM_BYTES),
        )(*found)

    rows = P(("dp", "seq"), None)
    return jax.shard_map(
        on_device, mesh=mesh, in_specs=(rows,) * 4 + (P(),), out_specs=(rows,) * 4, check_vma=False)
```

```python
import jax
import jax.numpy as jnp
from jax import lax
from jax.experimental import pallas as pl
from jax.experimental.pallas import tpu as pltpu
from jax.sharding import PartitionSpec as P

HEAD = 128
ROWS = 128
CHIP_ROWS = 2 * ROWS
GROUPS = 4
QCOLS = 1024
KCOLS = 512
SCALE = 168.0 ** (-0.5)
MASKED = -1e30
FAR = 2
FAR_BACK = 2
VMEM_BYTES = 62 << 20
MESH = pl.DeviceIdType.MESH
F32 = jnp.float32
BF16 = jnp.bfloat16


def dot_nn(a, b):
    return lax.dot_general(a, b, (((1,), (0,)), ((), ())), preferred_element_type=F32)


def dot_nt(a, b):
    return lax.dot_general(a, b, (((1,), (1,)), ((), ())), preferred_element_type=F32)


def dot_tn(a, b):
    return lax.dot_general(a, b, (((0,), (0,)), ((), ())), preferred_element_type=F32)


def make_kernel(dp_size, seq_size):
    chips = dp_size * seq_size // 2
    run = seq_size // 2

    def place(chip, core):
        rank = chip * 2 + core
        return {"dp": rank // seq_size, "seq": lax.rem(rank, seq_size)}

    def kernel(
        q_ref, k_ref, v_ref, do_ref, len_ref,
        att_o, dq_o, dk_o, dv_o,
        qw, dow, kw, vw, halo, bias,
        att_st, dq_st, kv_full, kv_sib, ret_st, ret, out_st,
        pass_h, pass_r,
        in_l, in_s, in_r, halo_s, halo_r, ret_s, ret_r,
        res_l, res_s, res_r, fin, pass_hs, pass_hr, pass_rs, pass_rr,
    ):
        rank = lax.axis_index("dp") * seq_size + lax.axis_index("seq")
        chip = rank // 2
        core = lax.rem(rank, 2)
        other = 1 - core
        nxt = lax.rem(chip + 1, chips)
        prv = lax.rem(chip + chips - 1, chips)
        sibling = place(chip, other)
        mine = pl.multiple_of(core * ROWS, ROWS)
        theirs = pl.multiple_of(other * ROWS, ROWS)

        line = chip // run
        even = lax.rem(line, 2) == 0
        src_wrap = lax.rem(chip, run) == run - 1
        dst_wrap = lax.rem(chip, run) == 0
        is_last = chip == chips - 1
        is_first = chip == 0
        sends_far = src_wrap & even & (line >= FAR)
        takes_far = dst_wrap & jnp.logical_not(even) & (line >= FAR_BACK)
        gets_far = dst_wrap & jnp.logical_not(even) & (line >= FAR)
        owed_far = src_wrap & even & (line >= FAR_BACK)
        passes_h = dst_wrap & even & (line >= FAR)
        passes_r = src_wrap & jnp.logical_not(even) & (line >= FAR_BACK)
        sends_near = jnp.logical_not(sends_far | is_last)
        takes_near = jnp.logical_not(takes_far | is_first)
        h_way = place(lax.rem(chip + chips - run + 1, chips), core)
        r_way = place(lax.rem(chip + run - 1, chips), core)
        h_from, h_to = lax.rem(chip + run - 1, chips), lax.rem(chip + run, chips)
        r_from, r_to = lax.rem(chip + chips - run + 1, chips), lax.rem(chip + chips - run, chips)

        barrier = pltpu.get_barrier_semaphore()

        def greet(*peers):
            for peer in peers:
                pl.semaphore_signal(barrier, inc=1, device_id=peer, device_id_type=MESH)

        greet(sibling)

        meets_nxt = jnp.logical_not(is_last | (sends_far & owed_far))
        meets_prv = jnp.logical_not(is_first | (takes_far & gets_far))

        @pl.when(meets_nxt)
        def _():
            greet(place(nxt, 0), place(nxt, 1))

        @pl.when(meets_prv)
        def _():
            greet(place(prv, 0), place(prv, 1))

        @pl.when(passes_h)
        def _():
            greet(place(h_from, core), place(h_to, 0), place(h_to, 1))

        @pl.when(passes_r)
        def _():
            greet(place(r_from, core), place(r_to, 0), place(r_to, 1))

        @pl.when(sends_far)
        def _():
            greet(h_way)

        @pl.when(owed_far)
        def _():
            back = lax.rem(chip + run, chips)
            greet(place(back, 0), place(back, 1))

        @pl.when(takes_far)
        def _():
            greet(r_way)

        @pl.when(gets_far)
        def _():
            ahead = lax.rem(chip + chips - run, chips)
            greet(place(ahead, 0), place(ahead, 1))

        operands = ((q_ref, qw, QCOLS), (do_ref, dow, QCOLS), (k_ref, kw, KCOLS), (v_ref, vw, KCOLS))

        def own_copy(i):
            src, dst, cols = operands[i]
            return pltpu.make_async_copy(
                src.at[:, pl.ds(pl.multiple_of(core * cols, cols), cols)],
                dst.at[pl.ds(mine, ROWS)], in_l.at[i])

        def sib_copy(i, rows):
            src, dst, cols = operands[i]
            return pltpu.make_async_remote_copy(
                src_ref=src.at[:, pl.ds(pl.multiple_of(other * cols, cols), cols)],
                dst_ref=dst.at[pl.ds(rows, ROWS)],
                send_sem=in_s.at[i], recv_sem=in_r.at[i],
                device_id=sibling, device_id_type=MESH)

        def halo_src(g, dest, kv):
            return (k_ref, v_ref)[kv].at[:, pl.ds(pl.multiple_of(dest * KCOLS + g * HEAD, HEAD), HEAD)]

        def halo_copy(g, dest, kv, rows, slot):
            return pltpu.make_async_remote_copy(
                src_ref=halo_src(g, dest, kv),
                dst_ref=halo.at[kv, g, pl.ds(rows, ROWS)],
                send_sem=halo_s.at[g, dest, kv], recv_sem=halo_r.at[g, slot, kv],
                device_id=place(nxt, dest), device_id_type=MESH)

        def ret_copy(g, dest, kv, slot):
            return pltpu.make_async_remote_copy(
                src_ref=ret_st.at[kv, g, pl.ds(dest * ROWS, ROWS)],
                dst_ref=ret.at[kv, slot, g],
                send_sem=ret_s.at[g, dest, kv], recv_sem=ret_r.at[g, slot, kv],
                device_id=place(prv, dest), device_id_type=MESH)

        def res_pairs(g, rows, half):
            cols = pl.multiple_of(half * QCOLS + g * 2 * HEAD, 2 * HEAD)
            return (
                (att_st.at[g, pl.ds(rows, ROWS)], att_o.at[:, pl.ds(cols, 2 * HEAD)]),
                (dq_st.at[g, pl.ds(rows, ROWS)], dq_o.at[:, pl.ds(cols, 2 * HEAD)]),
                (kv_full.at[0, g, pl.ds(rows, ROWS)], kv_sib.at[0, g]),
                (kv_full.at[1, g, pl.ds(rows, ROWS)], kv_sib.at[1, g]),
            )

        def res_remote(g, i, half):
            src, dst = res_pairs(g, theirs, half)[i]
            return pltpu.make_async_remote_copy(
                src_ref=src, dst_ref=dst, send_sem=res_s.at[g, i], recv_sem=res_r.at[g, i],
                device_id=sibling, device_id_type=MESH)

        def res_local(g, i):
            src, dst = res_pairs(g, mine, core)[i]
            return pltpu.make_async_copy(src, dst, res_l.at[g, i])

        for i in range(4):
            own_copy(i).start()

        @pl.when(is_first)
        def _():
            halo[...] = jnp.zeros_like(halo)

        @pl.when(is_last)
        def _():
            ret[...] = jnp.zeros_like(ret)

        def far_copy(g, dest, kv):
            return pltpu.make_async_remote_copy(
                src_ref=halo_src(g, dest, kv), dst_ref=pass_h.at[g, dest, kv],
                send_sem=halo_s.at[g, dest, kv], recv_sem=pass_hr.at[g, dest, kv],
                device_id=h_way, device_id_type=MESH)

        def far_ret(g, dest, kv):
            return pltpu.make_async_remote_copy(
                src_ref=ret_st.at[kv, g, pl.ds(dest * ROWS, ROWS)], dst_ref=pass_r.at[g, dest, kv],
                send_sem=ret_s.at[g, dest, kv], recv_sem=pass_rr.at[g, dest, kv],
                device_id=r_way, device_id_type=MESH)

        def on_halo(g, dest, kv):
            return pltpu.make_async_remote_copy(
                src_ref=pass_h.at[g, dest, kv], dst_ref=halo.at[kv, g, pl.ds(mine, ROWS)],
                send_sem=pass_hs.at[g, dest, kv], recv_sem=halo_r.at[g, core, kv],
                device_id=place(h_to, dest), device_id_type=MESH)

        def on_ret(g, dest, kv):
            return pltpu.make_async_remote_copy(
                src_ref=pass_r.at[g, dest, kv], dst_ref=ret.at[kv, core, g],
                send_sem=pass_rs.at[g, dest, kv], recv_sem=ret_r.at[g, core, kv],
                device_id=place(r_to, dest), device_id_type=MESH)

        def far_arrival(buf, sem, g, dest, kv):
            return pltpu.make_async_remote_copy(
                src_ref=buf.at[g, dest, kv], dst_ref=buf.at[g, dest, kv],
                send_sem=pass_hs.at[g, dest, kv], recv_sem=sem.at[g, dest, kv],
                device_id=sibling, device_id_type=MESH)

        pieces = [(dest, kv) for kv in range(2) for dest in range(2)]
        zero = jnp.int32(0)
        def some(count, cond):
            return jnp.where(cond, count, zero)

        expected = (
            1 + some(2, meets_nxt) + some(2, meets_prv) + some(3, passes_h) + some(3, passes_r)
            + some(1, sends_far) + some(2, owed_far) + some(1, takes_far) + some(2, gets_far))
        pl.semaphore_wait(barrier, expected)

        def send_halo(g):
            @pl.when(sends_near)
            def _():
                for kv in range(2):
                    for dest in range(2):
                        halo_copy(g, dest, kv, mine, core).start()

            @pl.when(sends_far)
            def _():
                for kv in range(2):
                    for dest in range(2):
                        far_copy(g, dest, kv).start()

        send_halo(0)
        for i in range(4):
            sib_copy(i, mine).start()

        @pl.loop(1, GROUPS)
        def _(g):
            send_halo(g)

        lane = lax.broadcasted_iota(jnp.int32, (8, 512), 1)
        ends = jnp.broadcast_to(len_ref[...], (8, 512)).astype(F32)
        step = 1
        while step < 512:
            ends = ends + jnp.where(lane >= step, pltpu.roll(ends, step, 1), 0.0)
            step *= 2
        base = (chip * CHIP_ROWS).astype(F32)
        row = lax.broadcasted_iota(jnp.int32, (CHIP_ROWS, CHIP_ROWS), 0)
        col = lax.broadcasted_iota(jnp.int32, (CHIP_ROWS, CHIP_ROWS), 1)
        position = lax.broadcasted_iota(jnp.int32, (CHIP_ROWS, 512), 0).astype(F32) + base
        ends_b = jnp.broadcast_to(ends[0:1], (CHIP_ROWS, 512))
        first = jnp.max(jnp.where(ends_b <= position, ends_b, 0.0), axis=1, keepdims=True) - base
        own = col <= row
        key_pos = jnp.where(own, col, col - CHIP_ROWS).astype(F32)
        bias[...] = jnp.where(key_pos >= first, 0.0, MASKED)

        for i in range(4):
            own_copy(i).wait()
        for i in range(4):
            copy = sib_copy(i, theirs)
            copy.wait_send()
            copy.wait_recv()

        @pl.loop(0, GROUPS)
        def _(g):
            @pl.when(passes_h & (g == 0))
            def _():
                for i in range(GROUPS):
                    for dest, kv in pieces:
                        far_arrival(pass_h, pass_hr, i, dest, kv).wait_recv()
                        on_halo(i, dest, kv).start()

            @pl.when(jnp.logical_not(is_first))
            def _():
                for slot in range(2):
                    for kv in range(2):
                        halo_copy(g, 0, kv, slot * ROWS, slot).wait_recv()

            kcols = pl.ds(pl.multiple_of(g * HEAD, HEAD), HEAD)
            k_own = kw[:, kcols]
            v_own = vw[:, kcols]
            k_halo = halo[0, g]
            v_halo = halo[1, g]
            sums = None
            for r in range(2):
                qcols = pl.ds(pl.multiple_of(g * 2 * HEAD + r * HEAD, HEAD), HEAD)
                qh = qw[:, qcols]
                gh = dow[:, qcols]
                score = jnp.where(own, dot_nt(qh, k_own), dot_nt(qh, k_halo)) * SCALE + bias[...]
                top = jnp.max(score, axis=1, keepdims=True)
                e = jnp.exp(score - top)
                prob = e / jnp.sum(e, axis=1, keepdims=True)
                w_own = jnp.where(own, prob, 0.0).astype(BF16)
                w_halo = jnp.where(own, 0.0, prob).astype(BF16)
                att = (dot_nn(w_own, v_own) + dot_nn(w_halo, v_halo)).astype(BF16)
                att_st[g, :, r * HEAD:(r + 1) * HEAD] = att
                delta = jnp.sum(gh.astype(F32) * att.astype(F32), axis=1, keepdims=True)
                dprob = jnp.where(own, dot_nt(gh, v_own), dot_nt(gh, v_halo))
                ds = prob * (dprob - delta) * SCALE
                ds_own = jnp.where(own, ds, 0.0).astype(BF16)
                ds_halo = jnp.where(own, 0.0, ds).astype(BF16)
                dq_st[g, :, r * HEAD:(r + 1) * HEAD] = dot_nn(ds_own, k_own) + dot_nn(ds_halo, k_halo)
                part = (dot_tn(ds_halo, qh), dot_tn(w_halo, gh), dot_tn(ds_own, qh), dot_tn(w_own, gh))
                sums = part if sums is None else tuple(a + b for a, b in zip(sums, part))
            ret_st[0, g] = sums[0].astype(BF16)
            ret_st[1, g] = sums[1].astype(BF16)

            @pl.when(takes_near)
            def _():
                for kv in range(2):
                    for dest in range(2):
                        ret_copy(g, dest, kv, core).start()

            @pl.when(takes_far)
            def _():
                for kv in range(2):
                    for dest in range(2):
                        far_ret(g, dest, kv).start()

            kv_full[0, g] = sums[2]
            kv_full[1, g] = sums[3]
            for i in range(4):
                res_remote(g, i, core).start()
            for i in range(2):
                res_local(g, i).start()

        @pl.when(passes_r)
        def _():
            @pl.loop(0, GROUPS)
            def _(g):
                for dest, kv in pieces:
                    far_arrival(pass_r, pass_rr, g, dest, kv).wait_recv()
                    on_ret(g, dest, kv).start()

        def fin_copy(g, half, kv):
            cols = pl.ds(pl.multiple_of(half * KCOLS + g * HEAD, HEAD), HEAD)
            return pltpu.make_async_copy(out_st.at[kv, half, g], (dk_o, dv_o)[kv].at[:, cols], fin.at[kv, half, g])

        @pl.loop(0, GROUPS)
        def _(g):
            for i in range(4):
                copy = res_remote(g, i, other)
                copy.wait_send()
                copy.wait_recv()
            for i in range(2):
                res_local(g, i).wait()

            @pl.when(jnp.logical_not(is_last))
            def _():
                for kv in range(2):
                    for dest in range(2):
                        halo_copy(g, dest, kv, mine, core).wait_send()
                    for slot in range(2):
                        ret_copy(g, slot, kv, slot).wait_recv()

            for kv in range(2):
                out_st[kv, core, g] = kv_full[kv, g, pl.ds(mine, ROWS)] + ret[kv, core, g].astype(F32)
                out_st[kv, other, g] = kv_sib[kv, g] + ret[kv, other, g].astype(F32)
                fin_copy(g, core, kv).start()
                fin_copy(g, other, kv).start()

        @pl.loop(0, GROUPS)
        def _(g):
            @pl.when(jnp.logical_not(is_first))
            def _():
                for kv in range(2):
                    for dest in range(2):
                        ret_copy(g, dest, kv, core).wait_send()

            for kv in range(2):
                for half in range(2):
                    fin_copy(g, half, kv).wait()

        @pl.when(passes_h)
        def _():
            @pl.loop(0, GROUPS)
            def _(g):
                for dest, kv in pieces:
                    on_halo(g, dest, kv).wait_send()

        @pl.when(passes_r)
        def _():
            @pl.loop(0, GROUPS)
            def _(g):
                for dest, kv in pieces:
                    on_ret(g, dest, kv).wait_send()

    return kernel


def hand_over(*refs):
    sources, targets, holds, sem_in, sem_out = refs[:4], refs[4:8], refs[8:12], refs[12], refs[13]
    parts = [(i, p) for p in range(4) for i in range(4)]

    def take(i, p):
        rows = pl.ds(p * (ROWS // 4), ROWS // 4)
        return pltpu.make_async_copy(sources[i].at[rows], holds[i].at[rows], sem_in.at[i, p])

    def give(i, p):
        rows = pl.ds(p * (ROWS // 4), ROWS // 4)
        return pltpu.make_async_copy(holds[i].at[rows], targets[i].at[rows], sem_out.at[i, p])

    for part in parts:
        take(*part).start()
    for part in parts:
        take(*part).wait()
        give(*part).start()
    for part in parts:
        give(*part).wait()


def solution(mesh):
    dp_size, seq_size = mesh.shape["dp"], mesh.shape["seq"]
    kernel = make_kernel(dp_size, seq_size)
    anyspace = pl.BlockSpec(memory_space=pl.ANY)
    in_hbm = pl.BlockSpec(memory_space=pltpu.HBM)
    dma = pltpu.SemaphoreType.DMA

    def on_device(queries, keys, values, output_gradient, doc_lengths):
        results = (
            jax.ShapeDtypeStruct((ROWS, 2048), BF16),
            jax.ShapeDtypeStruct((ROWS, 2048), F32),
            jax.ShapeDtypeStruct((ROWS, 1024), F32),
            jax.ShapeDtypeStruct((ROWS, 1024), F32),
        )
        found = pl.pallas_call(
            kernel,
            out_shape=results,
            in_specs=[in_hbm] * 4 + [pl.BlockSpec(memory_space=pltpu.VMEM)],
            out_specs=(anyspace,) * 4,
            scratch_shapes=[
                pltpu.VMEM((CHIP_ROWS, QCOLS), BF16),
                pltpu.VMEM((CHIP_ROWS, QCOLS), BF16),
                pltpu.VMEM((CHIP_ROWS, KCOLS), BF16),
                pltpu.VMEM((CHIP_ROWS, KCOLS), BF16),
                pltpu.VMEM((2, GROUPS, CHIP_ROWS, HEAD), BF16),
                pltpu.VMEM((CHIP_ROWS, CHIP_ROWS), F32),
                pltpu.VMEM((GROUPS, CHIP_ROWS, 2 * HEAD), BF16),
                pltpu.VMEM((GROUPS, CHIP_ROWS, 2 * HEAD), F32),
                pltpu.VMEM((2, GROUPS, CHIP_ROWS, HEAD), F32),
                pltpu.VMEM((2, GROUPS, ROWS, HEAD), F32),
                pltpu.VMEM((2, GROUPS, CHIP_ROWS, HEAD), BF16),
                pltpu.VMEM((2, 2, GROUPS, ROWS, HEAD), BF16),
                pltpu.VMEM((2, 2, GROUPS, ROWS, HEAD), F32),
                pltpu.VMEM((GROUPS, 2, 2, ROWS, HEAD), BF16),
                pltpu.VMEM((GROUPS, 2, 2, ROWS, HEAD), BF16),
                dma((4,)), dma((4,)), dma((4,)),
                dma((GROUPS, 2, 2)), dma((GROUPS, 2, 2)),
                dma((GROUPS, 2, 2)), dma((GROUPS, 2, 2)),
                dma((GROUPS, 2)), dma((GROUPS, 4)), dma((GROUPS, 4)),
                dma((2, 2, GROUPS)),
                dma((GROUPS, 2, 2)), dma((GROUPS, 2, 2)), dma((GROUPS, 2, 2)), dma((GROUPS, 2, 2)),
            ],
            compiler_params=pltpu.CompilerParams(
                collective_id=0, has_side_effects=True, vmem_limit_bytes=VMEM_BYTES),
        )(queries, keys, values, output_gradient, doc_lengths.reshape(1, -1))
        return pl.pallas_call(
            hand_over,
            out_shape=results,
            in_specs=[in_hbm] * 4,
            out_specs=(in_hbm,) * 4,
            scratch_shapes=[pltpu.VMEM(r.shape, r.dtype) for r in results] + [dma((4, 4)), dma((4, 4))],
            compiler_params=pltpu.CompilerParams(vmem_limit_bytes=VMEM_BYTES),
        )(*found)

    rows = P(("dp", "seq"), None)
    return jax.shard_map(
        on_device, mesh=mesh, in_specs=(rows,) * 4 + (P(),), out_specs=(rows,) * 4, check_vma=False)
```
